768 devices in a mesh: seq: 32 (over y_hi, x, core), mp: 24 (over z, y_lo).
Axes of the slice: x: 4, y: 8 (y_hi: 4, y_lo: 2; y = y_hi * 2 + y_lo), z: 12, core: 2. Of those that a mesh axis runs over, the one named last changes fastest.
Arguments:
- hidden_in: bfloat16 [16384, 5376], P('seq'), may hold values from -6 to 6
- norm_gain: float32 [5376], replicated, may hold values from 0.5 to 1.5
- query_weight: bfloat16 [5376, 3072], P(None, 'mp'), as said below
- kv_weight: bfloat16 [5376, 6144], P(None, 'mp'), as said below
- out_weight: bfloat16 [3072, 5376], P('mp'), may hold values from -0.875 to 0.875
Outputs:
- attn_out: bfloat16 [5376, 16384], P('mp', 'seq')
The draws below stay inside these ranges and needn't reach their ends.
Inputs may be any that keep to these rules, and one draw needn't show every extreme that they name: `query_weight`: query projection columns of mean zero scaled by the fan-in. `kv_weight`: key and value projection columns of mean zero; the columns of query heads 2j and 2j+1 are equal, one key-value head shared by the pair.
All inputs are finite; a program needn't handle non-finite values.
Results may differ from the reference program's by a relative error of at most 0.023.
Values may be sent and summed in bfloat16 or wider, within the bound.
A program may use at most 64 MiB of HBM per device.

```python
import math
import jax
import jax.numpy as jnp
from jax import lax

D = 5376
HD = 128
WINDOW = 1024
HQ = 24
KVH = 12
TOKENS = 16384


def paired_weights(key):
    scale_in = 1.0 / math.sqrt(D)
    query_part = jax.random.normal(jax.random.fold_in(key, 11), (D, HQ, HD), jnp.float32) * scale_in
    key_noise = jax.random.normal(jax.random.fold_in(key, 12), (D, KVH, HD), jnp.float32) * scale_in
    value_part = jax.random.normal(jax.random.fold_in(key, 13), (D, KVH, HD), jnp.float32) * scale_in
    key_part = key_noise
    stacked = jnp.stack([key_part, value_part], axis=2)
    doubled = jnp.repeat(stacked, 2, axis=1).reshape(D, HQ * 2 * HD)
    return (query_part.reshape(D, HQ * HD), doubled)


def draw_query_weight(key, part):
    return paired_weights(key)[0].astype(jnp.bfloat16)


def draw_kv_weight(key, part):
    return paired_weights(key)[1].astype(jnp.bfloat16)


def spiked(entries, rng, source, target, parts, factor):
    owner, partner = [(jnp.arange(entries.shape[dim]) // (entries.shape[dim] // parts)).reshape([-1 if axis == dim else 1 for axis in range(entries.ndim)]) for dim in (source, target)]
    chosen = jax.random.permutation(rng, parts)[partner]
    strong = (owner == chosen) | (owner == (partner + parts // 2) % parts)
    return jnp.where(strong, factor * entries, entries)


def block_levels(rng, dims, split, low, top_value):
    loudness, own = 1.0, jax.random.fold_in(rng, 6)
    for dim, parts in split:
        steps = jnp.exp(jax.random.uniform(jax.random.fold_in(own, dim), (parts,), jnp.float32, low / len(split), top_value / len(split)))
        loudness = loudness * jnp.repeat(steps, dims[dim] // parts).reshape([-1 if axis == dim else 1 for axis in range(len(dims))])
    return loudness


def bell_draw(stream_key, extent, spread, reach, shards=(), held_as=jnp.bfloat16):
    factor_of = block_levels(stream_key, extent, shards, -0.22, 0.18) if shards else 1.0
    values = jax.random.normal(stream_key, extent, jnp.float32) * spread * factor_of
    return jnp.minimum(jnp.maximum(values, -reach), reach).astype(held_as)


def noise_with(stream_key, extent, spread, bound, split, heavy, kind=jnp.bfloat16):
    array = spread * jax.random.normal(stream_key, extent, jnp.float32)
    if split:
        array = array * block_levels(stream_key, extent, split, -0.22, 0.18)
    return jnp.clip(spiked(array, jax.random.fold_in(stream_key, 3), *heavy), -bound, bound).astype(kind)


def setup_inputs(seed: int = 0) -> dict:
    key_list = jax.random.split(jax.random.key(seed), 6)
    return {
        "hidden_in": bell_draw(key_list[0], (TOKENS, D), 1.0, 6.0, ((0, 32),)),
        "norm_gain": jnp.clip(jax.random.uniform(key_list[1], (D,), jnp.float32, 0.5, 1.5), 0.5, 1.5),
        "query_weight": draw_query_weight(jax.random.fold_in(key_list[5], 71), 0),
        "kv_weight": draw_kv_weight(jax.random.fold_in(key_list[5], 71), 0),
        "out_weight": noise_with(key_list[4], (HQ * HD, D), HD ** -0.5, 0.875, ((0, 24),), (0, 1, 24, 2.25)),
    }


def rotate_half(tensor, positions):
    half = tensor.shape[-1] // 2
    freq = jnp.exp(-math.log(10000.0) * jnp.arange(half, dtype=jnp.float32) * (2.0 / tensor.shape[-1]))
    angle = positions[:, None, None] * freq[None, None, :]
    cosine = jnp.cos(angle)
    sine = jnp.sin(angle)
    first = tensor[..., :half]
    second = tensor[..., half:]
    return jnp.concatenate([first * cosine - second * sine, second * cosine + first * sine], axis=-1)

def reference(hidden_in, norm_gain, query_weight, kv_weight, out_weight):
    length = hidden_in.shape[0]
    widths = hidden_in.astype(jnp.float32)
    inverse = lax.rsqrt(lax.optimization_barrier(jnp.mean(widths * widths, axis=-1, keepdims=True)) + 1e-06)
    normed = (widths * inverse * norm_gain.astype(jnp.float32)[None, :]).astype(jnp.bfloat16)
    positions = jnp.arange(length).astype(jnp.float32)
    queries = jnp.dot(normed, query_weight, preferred_element_type=jnp.float32).reshape(length, HQ, HD)
    queries = rotate_half(queries, positions).astype(jnp.bfloat16)
    projected = jnp.dot(normed, kv_weight, preferred_element_type=jnp.float32).reshape(length, HQ, 2, HD)
    keys = rotate_half(projected[:, :, 0, :], positions).astype(jnp.bfloat16)
    values = projected[:, :, 1, :].astype(jnp.bfloat16)
    block = math.gcd(length, 512)
    pad_keys = jnp.concatenate([jnp.zeros((WINDOW, HQ, HD), jnp.bfloat16), keys], axis=0)
    pad_values = jnp.concatenate([jnp.zeros((WINDOW, HQ, HD), jnp.bfloat16), values], axis=0)

    def one_block(index):
        offset = (index * block).astype(jnp.int32)
        query_block = lax.dynamic_slice_in_dim(queries, offset, block, 0)
        key_block = lax.dynamic_slice_in_dim(pad_keys, offset, WINDOW + block, 0)
        value_block = lax.dynamic_slice_in_dim(pad_values, offset, WINDOW + block, 0)
        scores = jnp.einsum('qhd,khd->hqk', query_block.astype(jnp.float32), key_block.astype(jnp.float32))
        scores = scores * (1.0 / math.sqrt(168.0))
        query_pos = offset + jnp.arange(block, dtype=jnp.int32)
        key_pos = offset - WINDOW + jnp.arange(WINDOW + block, dtype=jnp.int32)
        valid = (key_pos[None, :] <= query_pos[:, None]) & (query_pos[:, None] - key_pos[None, :] < WINDOW) & (key_pos[None, :] >= 0)
        scores = jnp.where(valid[None], scores, jnp.float32(-1e+30))
        highest = lax.optimization_barrier(jnp.max(scores, axis=-1, keepdims=True))
        expo = jnp.exp(scores - highest)
        probs = (expo / lax.optimization_barrier(jnp.sum(expo, axis=-1, keepdims=True))).astype(jnp.bfloat16)
        mixed = jnp.einsum('hqk,khd->qhd', probs.astype(jnp.float32), value_block.astype(jnp.float32))
        return mixed.astype(jnp.bfloat16).reshape(block, HQ * HD)
    head_out = lax.map(one_block, jnp.arange(length // block, dtype=jnp.int32)).reshape(length, HQ * HD)

    def add_head(total, head):
        start_col = (head * HD).astype(jnp.int32)
        part_out = lax.dynamic_slice_in_dim(head_out, start_col, HD, 1)
        part_weight = lax.dynamic_slice_in_dim(out_weight, start_col, HD, 0)
        term = jnp.dot(part_out, part_weight, preferred_element_type=jnp.float32).astype(jnp.bfloat16)
        term = lax.optimization_barrier(term)
        return (total + term.astype(jnp.float32), None)
    summed, unused = lax.scan(add_head, jnp.zeros((length, D), jnp.float32), jnp.arange(HQ, dtype=jnp.int32))
    return summed.T.astype(jnp.bfloat16)
```

```python
import math

import jax
import jax.numpy as jnp
from jax import lax
from jax.experimental import pallas as pl
from jax.experimental.pallas import tpu as pltpu
from jax.sharding import PartitionSpec as P

MESH = pl.DeviceIdType.MESH
BF = jnp.bfloat16
F32 = jnp.float32

D = 5376
HD = 128
WINDOW = 1024
ROWS = 512
NZ = 12
NX = 4
HALF = NZ // 2
FEATS = D // NZ
MINE = FEATS // 2
QUARTER = FEATS // NX
NK = 7
KC = D // NK
NB = 4
BLK = ROWS // NB
KEYS = WINDOW + BLK
SCALE = math.log2(math.e) / math.sqrt(168.0)

NT = (((1,), (1,)), ((), ()))


def kernel(
    x_hbm, gain_ref, wq_hbm, wkv_hbm, wo_hbm, cos_ref, sin_ref, out_ref,
    xb, xg, wqb, wkvb, wob, wt, wbuf, kv, qb, ho, acc, ss, rc, rs, psend, precv, own,
    ld_x, ld_kv, ld_q, ld_o,
    a_s, a_r, b_s, b_r, c1_s, c1_r, c2_s, c2_r,
    p1_s, p1_r, p2_s, p2_r, p3_s, p3_r,
    r_s, l_s, g_r, y_s, y_r,
):
    s = lax.axis_index("seq")
    m = lax.axis_index("mp")
    nseq = lax.axis_size("seq")
    z = m // 2
    yl = m % 2
    core = s % 2
    x = (s // 2) % NX
    partner = m + 1 - 2 * yl
    sibling = s + 1 - 2 * core
    has_prev = s >= 2
    has_next = s < nseq - 2

    def at_z(dist):
        return ((z + dist + NZ) % NZ) * 2 + yl

    def at_x(dist):
        return s + 2 * ((x + dist) % NX - x)

    def copy(src, dst, ssem, rsem, seq, mp):
        return pltpu.make_async_remote_copy(
            src_ref=src, dst_ref=dst, send_sem=ssem, recv_sem=rsem,
            device_id=(seq, mp), device_id_type=MESH,
        )

    load_o = pltpu.make_async_copy(wo_hbm, wob, ld_o)
    load_o.start()
    loads = []
    for k in range(NK):
        lx = pltpu.make_async_copy(x_hbm.at[:, pl.ds(k * KC, KC)], xb.at[k], ld_x.at[k])
        lkv = pltpu.make_async_copy(wkv_hbm.at[pl.ds(k * KC, KC), :], wkvb.at[k], ld_kv.at[k])
        lx.start()
        lkv.start()
        loads.append((lx, lkv))
    load_q = pltpu.make_async_copy(wq_hbm, wqb, ld_q)
    load_q.start()

    barrier = pltpu.get_barrier_semaphore()

    def greet(seq, mp):
        pl.semaphore_signal(barrier, inc=1, device_id=(seq, mp), device_id_type=MESH)

    for dist in range(1, NZ):
        greet(s, at_z(dist))
    for dist in range(1, NX):
        greet(at_x(dist), m)
    greet(sibling, m)
    greet(s, partner)

    @pl.when(has_prev)
    def _():
        greet(s - 2, m)

    @pl.when(has_next)
    def _():
        greet(s + 2, m)

    lane = lax.broadcasted_iota(jnp.int32, (32, HD), 1)
    sign = jnp.where(lane < HD // 2, -1.0, 1.0).astype(F32)
    cos_low = cos_ref[16:48, :]
    sin_low = sin_ref[16:48, :]
    for a in range(16):
        cos_high = cos_ref[a : a + 1, :]
        sin_high = sin_ref[a : a + 1, :]
        rc[32 * a : 32 * a + 32, :] = cos_high * cos_low - sin_high * sin_low
        rs[32 * a : 32 * a + 32, :] = (sin_high * cos_low + cos_high * sin_low) * sign

    @pl.when(s == 0)
    def _():
        kv[:, 0 : 2 * ROWS, :] = jnp.zeros((2, 2 * ROWS, HD), BF)

    @pl.when(s == 1)
    def _():
        kv[:, 0:ROWS, :] = jnp.zeros((2, ROWS, HD), BF)

    load_o.wait()
    for f in range(D // HD):
        wt[f * HD : (f + 1) * HD, :] = wob[:, f * HD : (f + 1) * HD].T

    def scale(k):
        for r in range(0, ROWS, 16):
            wide = xb[k, r : r + 16, :].astype(F32)
            square = wide * wide
            part = square[:, 0:HD]
            for c in range(HD, KC, HD):
                part = part + square[:, c : c + HD]
            if k == 0:
                ss[r : r + 16, :] = part
            else:
                ss[r : r + 16, :] += part
            xg[k, r : r + 16, :] = (wide * gain_ref[:, k * KC : (k + 1) * KC]).astype(BF)

    loads[0][0].wait()
    loads[0][1].wait()
    scale(0)
    for k in range(NK):
        if k + 1 < NK:
            loads[k + 1][0].wait()
            loads[k + 1][1].wait()
            scale(k + 1)
        part = jnp.dot(xg[k], wkvb[k], preferred_element_type=F32)
        if k == 0:
            acc[...] = part
        else:
            acc[...] += part
    inverse = lax.rsqrt(jnp.sum(ss[...], axis=1, keepdims=True) * (1.0 / D) + 1e-06)

    def rope(t):
        return t * rc[...] + pltpu.roll(t, HD // 2, 1) * rs[...]

    kv[0, 2 * ROWS : 3 * ROWS, :] = rope(acc[:, 0:HD] * inverse).astype(BF)
    kv[1, 2 * ROWS : 3 * ROWS, :] = (acc[:, HD : 2 * HD] * inverse).astype(BF)

    pl.semaphore_wait(
        barrier,
        (NZ - 1) + (NX - 1) + 2 + has_prev.astype(jnp.int32) + has_next.astype(jnp.int32),
    )

    def copy_a(j):
        return copy(
            kv.at[yl, pl.ds(2 * ROWS + j * BLK, BLK), :], kv.at[yl, pl.ds(j * BLK, BLK), :],
            a_s.at[j], a_r.at[j], s + 2, m,
        )

    def copy_b(j, half):
        block = kv.at[half, pl.ds(j * BLK, BLK), :]
        return copy(block, block, b_s.at[j], b_r.at[j], s, partner)

    def copy_c1():
        return copy(
            kv.at[:, pl.ds(2 * ROWS, ROWS), :], kv.at[:, pl.ds(ROWS, ROWS), :],
            c1_s.at[0], c1_r.at[0], sibling, m,
        )

    def copy_c2(j, half):
        return copy(
            kv.at[half, pl.ds(j * BLK, BLK), :], kv.at[half, pl.ds(ROWS + j * BLK, BLK), :],
            c2_s.at[half, j], c2_r.at[half, j], sibling, m,
        )

    order = tuple(range(NB - 1, -1, -1))

    @pl.when(has_next)
    def _():
        for j in order:
            copy_a(j).start()

    @pl.when(core == 0)
    def _():
        copy_c1().start()

    def copy_p1(j):
        dist = (j + 1) * (1 - 2 * core)
        plane = (z + dist + NZ) % NZ
        slot = 1 + j + HALF * core
        return copy(
            wt.at[pl.ds(pl.multiple_of(plane * FEATS + x * QUARTER, 16), QUARTER), :],
            wbuf.at[slot, pl.ds(pl.multiple_of(x * QUARTER, 16), QUARTER), :],
            p1_s.at[j], p1_r.at[j], s, plane * 2 + yl,
        )

    for j in range(HALF):
        copy_p1(j).start()
    wbuf[0] = wt[pl.ds(pl.multiple_of(z * FEATS, 16), FEATS), :]

    load_q.wait()
    queries = jnp.dot(xg[0], wqb[0:KC, :], preferred_element_type=F32)
    for k in range(1, NK):
        queries = queries + jnp.dot(
            xg[k], wqb[k * KC : (k + 1) * KC, :], preferred_element_type=F32
        )
    qb[...] = (rope(queries * inverse) * SCALE).astype(BF)

    @pl.when(has_prev & (core == 1))
    def _():
        for j in order:
            copy_a(j).wait_recv()
            copy_b(j, yl).start()
            copy_c2(j, yl).start()
        for j in order:
            copy_b(j, 1 - yl).wait_recv()
            copy_c2(j, 1 - yl).start()

    @pl.when(has_prev & (core == 0))
    def _():
        for j in order:
            copy_a(j).wait_recv()
            copy_b(j, yl).start()
        for j in order:
            copy_b(j, 1 - yl).wait_recv()
            copy_c2(j, yl).wait_recv()
            copy_c2(j, 1 - yl).wait_recv()

    @pl.when(core == 1)
    def _():
        copy_c1().wait_recv()

    right, left = at_z(1), at_z(-1)

    def send_right(b, d):
        return copy(ho.at[b, d], ho.at[b, d + 1], r_s.at[b, d], g_r.at[b, d + 1], s, right)

    def send_left(b, e):
        to = HALF if e == HALF - 1 else HALF + e + 1
        frm = 0 if e == 0 else HALF + e
        return copy(ho.at[b, frm], ho.at[b, to], l_s.at[b, e], g_r.at[b, to], s, left)

    first_key = jnp.maximum(WINDOW - ROWS * s, 0)
    query_row = lax.broadcasted_iota(jnp.int32, (BLK, KEYS), 0)
    key_row = lax.broadcasted_iota(jnp.int32, (BLK, KEYS), 1)
    band = (key_row > query_row) & (key_row <= query_row + WINDOW)
    for b in order:
        start = b * BLK
        scores = lax.dot_general(
            qb[start : start + BLK, :], kv[0, start : start + KEYS, :], NT,
            preferred_element_type=F32,
        )
        scores = jnp.where(band & (key_row + start >= first_key), scores, -1e30)
        weights = jnp.exp2(scores - jnp.max(scores, axis=1, keepdims=True))
        total = jnp.sum(weights, axis=1, keepdims=True)
        mixed = jnp.dot(
            weights.astype(BF), kv[1, start : start + KEYS, :], preferred_element_type=F32
        )
        ho[b, 0] = (mixed / total).astype(BF)
        send_right(b, 0).start()
        send_left(b, 0).start()

    def quarter(slot, dist):
        rows = pl.ds(pl.multiple_of(((x - dist + NX) % NX) * QUARTER, 16), QUARTER)
        return wbuf.at[pl.ds(slot, HALF), rows, :]

    mine = 1 + HALF * core
    other = 1 + HALF * (1 - core)

    def copy_p2(dist):
        return copy(quarter(mine, 0), quarter(mine, 0), p2_s.at[dist], p2_r.at[dist], at_x(dist), m)

    def arrival_p2(dist):
        return copy(quarter(mine, dist), quarter(mine, dist), p2_s.at[dist], p2_r.at[dist], at_x(-dist), m)

    def copy_sib(dist, slot):
        return copy(quarter(slot, dist), quarter(slot, dist), p3_s.at[dist], p3_r.at[dist], sibling, m)

    for j in range(HALF):
        copy_p1(j).wait_recv()
    for dist in range(1, NX):
        copy_p2(dist).start()
    copy_sib(0, mine).start()

    for hop in range(1, HALF):
        for b in order:
            send_right(b, hop - 1).wait_recv()
            if hop + 1 < HALF or b < NB // 2:
                send_right(b, hop).start()
            send_left(b, hop - 1).wait_recv()
            if hop + 1 < HALF or b >= NB // 2:
                send_left(b, hop).start()
        if hop == 3:
            for dist in range(1, NX):
                arrival_p2(dist).wait_recv()
                copy_sib(dist, mine).start()
    for dist in range(NX):
        copy_sib(dist, other).wait_recv()

    def copy_y(b):
        return copy(psend.at[b], precv.at[b], y_s.at[b], y_r.at[b], s, partner)

    theirs_at = pl.multiple_of((1 - yl) * MINE, 16)
    mine_at = pl.multiple_of(yl * MINE, 16)

    def product(heads, at):
        rows = jnp.concatenate([wbuf[i, pl.ds(at, MINE), :] for i in range(NZ)], axis=1)
        return lax.dot_general(rows, heads, NT, preferred_element_type=F32)

    for b in order:
        if b < NB // 2:
            send_right(b, HALF - 1).wait_recv()
        else:
            send_left(b, HALF - 1).wait_recv()
        heads = jnp.concatenate([ho[b, i] for i in range(NZ)], axis=1)
        psend[b] = product(heads, theirs_at).astype(BF)
        copy_y(b).start()
        own[b] = product(heads, mine_at)
    for b in order:
        copy_y(b).wait_recv()
        out_ref[:, b * BLK : (b + 1) * BLK] = (own[b] + precv[b].astype(F32)).astype(BF)

    @pl.when(has_next)
    def _():
        for j in order:
            copy_a(j).wait_send()

    @pl.when(core == 0)
    def _():
        copy_c1().wait_send()

    @pl.when(has_prev)
    def _():
        for j in order:
            copy_b(j, yl).wait_send()

    @pl.when(has_prev & (core == 1))
    def _():
        for j in order:
            copy_c2(j, yl).wait_send()
            copy_c2(j, 1 - yl).wait_send()

    for j in range(HALF):
        copy_p1(j).wait_send()
    for dist in range(1, NX):
        copy_p2(dist).wait_send()
    for dist in range(NX):
        copy_sib(dist, mine).wait_send()
    for b in order:
        for hop in range(HALF):
            if hop + 1 < HALF or b < NB // 2:
                send_right(b, hop).wait_send()
            if hop + 1 < HALF or b >= NB // 2:
                send_left(b, hop).wait_send()
        copy_y(b).wait_send()


def per_device(hidden_in, norm_gain, query_weight, kv_weight, out_weight):
    first = (lax.axis_index("seq") * ROWS).astype(F32)
    row = jnp.arange(48, dtype=jnp.int32)
    place = jnp.where(row < 16, first + 32.0 * row.astype(F32), (row - 16).astype(F32))
    index = (jnp.arange(HD, dtype=jnp.int32) % (HD // 2)).astype(F32)
    angle = place[:, None] * jnp.exp(-math.log(10000.0) * index * (2.0 / HD))[None, :]
    any_space = pl.BlockSpec(memory_space=pl.ANY)
    vmem = pl.BlockSpec(memory_space=pltpu.VMEM)
    dma = pltpu.SemaphoreType.DMA
    return pl.pallas_call(
        kernel,
        out_shape=jax.ShapeDtypeStruct((MINE, ROWS), BF),
        in_specs=[any_space, vmem, any_space, any_space, any_space, vmem, vmem],
        out_specs=vmem,
        scratch_shapes=[
            pltpu.VMEM((NK, ROWS, KC), BF),
            pltpu.VMEM((NK, ROWS, KC), BF),
            pltpu.VMEM((D, HD), BF),
            pltpu.VMEM((NK, KC, 2 * HD), BF),
            pltpu.VMEM((HD, D), BF),
            pltpu.VMEM((D, HD), BF),
            pltpu.VMEM((NZ + 1, FEATS, HD), BF),
            pltpu.VMEM((2, 3 * ROWS, HD), BF),
            pltpu.VMEM((ROWS, HD), BF),
            pltpu.VMEM((NB, NZ, BLK, HD), BF),
            pltpu.VMEM((ROWS, 2 * HD), F32),
            pltpu.VMEM((ROWS, HD), F32),
            pltpu.VMEM((ROWS, HD), F32),
            pltpu.VMEM((ROWS, HD), F32),
            pltpu.VMEM((NB, MINE, BLK), BF),
            pltpu.VMEM((NB, MINE, BLK), BF),
            pltpu.VMEM((NB, MINE, BLK), F32),
            dma((NK,)), dma((NK,)), dma, dma,
            dma((NB,)), dma((NB,)), dma((NB,)), dma((NB,)),
            dma((1,)), dma((1,)), dma((2, NB)), dma((2, NB)),
            dma((HALF,)), dma((HALF,)), dma((NX,)), dma((NX,)), dma((NX,)), dma((NX,)),
            dma((NB, HALF)), dma((NB, HALF)), dma((NB, NZ)), dma((NB,)), dma((NB,)),
        ],
        compiler_params=pltpu.CompilerParams(
            collective_id=0, has_side_effects=True, vmem_limit_bytes=60 * 1024 * 1024
        ),
    )(
        hidden_in, norm_gain.reshape(1, D), query_weight, kv_weight, out_weight,
        jnp.cos(angle), jnp.sin(angle),
    )


def solution(mesh):
    in_specs = (P("seq", None), P(), P(None, "mp"), P(None, "mp"), P("mp", None))
    out_specs = P("mp", "seq")
    return jax.shard_map(
        per_device, mesh=mesh, in_specs=in_specs, out_specs=out_specs, check_vma=False
    )
```

```python
import math

import jax
import jax.numpy as jnp
import numpy as np
from jax import lax
from jax.experimental import pallas as pl
from jax.experimental.pallas import tpu as pltpu
from jax.sharding import PartitionSpec as P

MESH = pl.DeviceIdType.MESH
BF = jnp.bfloat16
F32 = jnp.float32

D = 5376
HD = 128
WINDOW = 1024
ROWS = 512
NZ = 12
NX = 4
HALF = NZ // 2
FEATS = D // NZ
MINE = FEATS // 2
QUARTER = FEATS // NX
NK = 7
KC = D // NK
AHEAD = 4
NB = 4
BLK = ROWS // NB
KEYS = WINDOW + BLK
SCALE = math.log2(math.e) / math.sqrt(168.0)

NT = (((1,), (1,)), ((), ()))


def kernel(
    x_hbm, gain_ref, wq_hbm, wkv_hbm, wo_hbm, freq_ref, out_ref,
    xb, xg, wqb, wkvb, wob, wt, wbuf, kv, qb, ho, acc, ss, rc, rs, psend, precv, own, rel,
    ld_x, ld_kv, ld_q, ld_o,
    a_s, a_r, b_s, b_r, c1_s, c1_r, c2_s, c2_r,
    p1_s, p1_r, p2_s, p2_r, p3_s, p3_r,
    r_s, l_s, g_r, y_s, y_r, f_s, f_r,
):
    s = lax.axis_index("seq")
    m = lax.axis_index("mp")
    nseq = lax.axis_size("seq")
    z = m // 2
    yl = m % 2
    core = s % 2
    x = (s // 2) % NX
    partner = m + 1 - 2 * yl
    sibling = s + 1 - 2 * core
    has_prev = s >= 2
    has_next = s < nseq - 2
    turns = x == NX - 1
    passes = (x == 0) & (s < nseq - 2 * NX) & (yl == 1)
    passed = (x == 0) & has_prev & (yl == 0)

    def at_z(dist):
        return ((z + dist + NZ) % NZ) * 2 + yl

    def at_x(dist):
        return s + 2 * ((x + dist) % NX - x)

    def copy(src, dst, ssem, rsem, seq, mp):
        return pltpu.make_async_remote_copy(
            src_ref=src, dst_ref=dst, send_sem=ssem, recv_sem=rsem,
            device_id=(seq, mp), device_id_type=MESH,
        )

    load_o = pltpu.make_async_copy(wo_hbm, wob, ld_o)
    load_q = pltpu.make_async_copy(wq_hbm, wqb, ld_q)

    def load_x(k):
        return pltpu.make_async_copy(x_hbm.at[:, pl.ds(k * KC, KC)], xb.at[k], ld_x.at[k])

    def load_kv(k):
        return pltpu.make_async_copy(wkv_hbm.at[pl.ds(k * KC, KC), :], wkvb.at[k], ld_kv.at[k])

    def load(k):
        if k < NK:
            load_x(k).start()
            load_kv(k).start()
        elif k == NK:
            load_o.start()
        elif k == NK + 1:
            load_q.start()

    for k in range(AHEAD):
        load(k)

    barrier = pltpu.get_barrier_semaphore()

    def greet(seq, mp):
        pl.semaphore_signal(barrier, inc=1, device_id=(seq, mp), device_id_type=MESH)

    for dist in range(1, NZ):
        greet(s, at_z(dist))
    for dist in range(1, NX):
        greet(at_x(dist), m)
    greet(sibling, m)
    greet(s, partner)

    @pl.when(has_prev)
    def _():
        greet(s - 2, m)

    @pl.when(has_next)
    def _():
        greet(s + 2, m)

    @pl.when(passes)
    def _():
        greet(s + 2 * NX, m - 1)

    @pl.when(passed)
    def _():
        greet(s - 2 * NX, m + 1)

    lane = lax.broadcasted_iota(jnp.int32, (32, HD), 1)
    sign = jnp.where(lane < HD // 2, -1.0, 1.0).astype(F32)
    row = lax.broadcasted_iota(jnp.int32, (48, HD), 0)
    place = jnp.where(row < 16, ROWS * s + 32 * row, row - 16).astype(F32)
    angle = place * freq_ref[...]
    cosine = jnp.cos(angle)
    sine = jnp.sin(angle)
    cos_low = cosine[16:48, :]
    sin_low = sine[16:48, :]
    for a in range(16):
        cos_high = cosine[a : a + 1, :]
        sin_high = sine[a : a + 1, :]
        rc[32 * a : 32 * a + 32, :] = cos_high * cos_low - sin_high * sin_low
        rs[32 * a : 32 * a + 32, :] = (sin_high * cos_low + cos_high * sin_low) * sign

    @pl.when(s == 0)
    def _():
        kv[:, 0 : 2 * ROWS, :] = jnp.zeros((2, 2 * ROWS, HD), BF)

    @pl.when(s == 1)
    def _():
        kv[:, 0:ROWS, :] = jnp.zeros((2, ROWS, HD), BF)

    def scale(k):
        gain = gain_ref[pl.ds(k * KC, KC)].reshape(1, KC)
        for r in range(0, ROWS, 16):
            wide = xb[k, r : r + 16, :].astype(F32)
            square = wide * wide
            part = square[:, 0:HD]
            for c in range(HD, KC, HD):
                part = part + square[:, c : c + HD]
            if k == 0:
                ss[r : r + 16, :] = part
            else:
                ss[r : r + 16, :] += part
            xg[k, r : r + 16, :] = (wide * gain).astype(BF)

    def arrive(k):
        load_x(k).wait()
        load_kv(k).wait()
        load(k + AHEAD)

    arrive(0)
    scale(0)
    for k in range(NK):
        if k + 1 < NK:
            arrive(k + 1)
            scale(k + 1)
        part = jnp.dot(xg[k], wkvb[k], preferred_element_type=F32)
        if k == 0:
            acc[...] = part
        else:
            acc[...] += part
    inverse = lax.rsqrt(jnp.sum(ss[...], axis=1, keepdims=True) * (1.0 / D) + 1e-06)

    def rope(t):
        return t * rc[...] + pltpu.roll(t, HD // 2, 1) * rs[...]

    kv[0, 2 * ROWS : 3 * ROWS, :] = rope(acc[:, 0:HD] * inverse).astype(BF)
    kv[1, 2 * ROWS : 3 * ROWS, :] = (acc[:, HD : 2 * HD] * inverse).astype(BF)

    pl.semaphore_wait(
        barrier,
        (NZ - 1) + (NX - 1) + 2 + has_prev.astype(jnp.int32) + has_next.astype(jnp.int32)
        + passes.astype(jnp.int32) + passed.astype(jnp.int32),
    )

    def copy_a(j):
        return copy(
            kv.at[yl, pl.ds(2 * ROWS + j * BLK, BLK), :], kv.at[yl, pl.ds(j * BLK, BLK), :],
            a_s.at[j], a_r.at[j], s + 2, m,
        )

    def copy_b(j, half):
        block = kv.at[half, pl.ds(j * BLK, BLK), :]
        return copy(block, block, b_s.at[j], b_r.at[j], s, partner)

    def copy_c1():
        return copy(
            kv.at[:, pl.ds(2 * ROWS, ROWS), :], kv.at[:, pl.ds(ROWS, ROWS), :],
            c1_s.at[0], c1_r.at[0], sibling, m,
        )

    def copy_c2(j, half):
        return copy(
            kv.at[half, pl.ds(j * BLK, BLK), :], kv.at[half, pl.ds(ROWS + j * BLK, BLK), :],
            c2_s.at[half, j], c2_r.at[half, j], sibling, m,
        )

    order = tuple(range(NB - 1, -1, -1))

    def copy_in(j):
        return copy(
            kv.at[0, pl.ds(2 * ROWS + j * BLK, BLK), :], rel.at[j], f_s.at[0, j], f_r.at[j], at_x(1), m,
        )

    def copy_on(j):
        return copy(
            rel.at[j], kv.at[0, pl.ds(j * BLK, BLK), :], f_s.at[1, j], a_r.at[j], s + 2 * NX, m - 1,
        )

    straight = has_next & (jnp.logical_not(turns) | (yl == 1))
    around = has_next & turns & (yl == 1)

    def send_on(which):
        @pl.when(straight)
        def _():
            for j in which:
                copy_a(j).start()

        @pl.when(around)
        def _():
            for j in which:
                copy_in(j).start()

    @pl.when(core == 1)
    def _():
        send_on(order)

    @pl.when(core == 0)
    def _():
        send_on(order[:1])
        copy_c1().start()

    load_o.wait()
    for f in range(D // HD):
        wt[f * HD : (f + 1) * HD, :] = wob[:, f * HD : (f + 1) * HD].T

    def copy_p1(j):
        dist = (j + 1) * (1 - 2 * core)
        plane = (z + dist + NZ) % NZ
        slot = 1 + j + HALF * core
        return copy(
            wt.at[pl.ds(pl.multiple_of(plane * FEATS + x * QUARTER, 16), QUARTER), :],
            wbuf.at[slot, pl.ds(pl.multiple_of(x * QUARTER, 16), QUARTER), :],
            p1_s.at[j], p1_r.at[j], s, plane * 2 + yl,
        )

    for j in range(HALF):
        copy_p1(j).start()
    wbuf[0] = wt[pl.ds(pl.multiple_of(z * FEATS, 16), FEATS), :]

    load_q.wait()
    queries = jnp.dot(xg[0], wqb[0:KC, :], preferred_element_type=F32)
    for k in range(1, NK):
        queries = queries + jnp.dot(
            xg[k], wqb[k * KC : (k + 1) * KC, :], preferred_element_type=F32
        )
    qb[...] = (rope(queries * inverse) * SCALE).astype(BF)

    @pl.when(core == 0)
    def _():
        send_on(order[1:])

    @pl.when(passes)
    def _():
        for j in order:
            copy_in(j).wait_recv()
            copy_on(j).start()

    @pl.when(has_prev & (core == 1))
    def _():
        for j in order:
            copy_a(j).wait_recv()
            copy_b(j, yl).start()
            copy_c2(j, yl).start()
        for j in order:
            copy_b(j, 1 - yl).wait_recv()
            copy_c2(j, 1 - yl).start()

    @pl.when(has_prev & (core == 0))
    def _():
        for j in order:
            copy_a(j).wait_recv()
            copy_b(j, yl).start()
        for j in order:
            copy_c2(j, yl).wait_recv()
            copy_c2(j, 1 - yl).wait_recv()

    @pl.when(core == 1)
    def _():
        copy_c1().wait_recv()

    right, left = at_z(1), at_z(-1)

    def send_right(b, d):
        return copy(ho.at[b, d], ho.at[b, d + 1], r_s.at[b, d], g_r.at[b, d + 1], s, right)

    def send_left(b, e):
        to = HALF if e == HALF - 1 else HALF + e + 1
        frm = 0 if e == 0 else HALF + e
        return copy(ho.at[b, frm], ho.at[b, to], l_s.at[b, e], g_r.at[b, to], s, left)

    first_key = jnp.maximum(WINDOW - ROWS * s, 0)
    query_row = lax.broadcasted_iota(jnp.int32, (BLK, BLK), 0)
    key_row = lax.broadcasted_iota(jnp.int32, (BLK, BLK), 1)
    column = lax.broadcasted_iota(jnp.int32, (1, KEYS), 1)
    for b in order:
        start = b * BLK

        @pl.when(has_prev & (core == 0))
        def _():
            copy_b(b, 1 - yl).wait_recv()

        scores = lax.dot_general(
            qb[start : start + BLK, :], kv[0, start : start + KEYS, :], NT,
            preferred_element_type=F32,
        )
        exists = column + start >= first_key
        scores = jnp.where(exists, scores, -1e30)
        scores = jnp.concatenate(
            [
                jnp.where(key_row > query_row, scores[:, 0:BLK], -1e30),
                scores[:, BLK:WINDOW],
                jnp.where(key_row <= query_row, scores[:, WINDOW:KEYS], -1e30),
            ],
            axis=1,
        )
        weights = jnp.exp2(scores - jnp.max(scores, axis=1, keepdims=True))
        total = jnp.sum(weights, axis=1, keepdims=True)
        mixed = jnp.dot(
            weights.astype(BF), kv[1, start : start + KEYS, :], preferred_element_type=F32
        )
        ho[b, 0] = (mixed / total).astype(BF)
        send_right(b, 0).start()
        send_left(b, 0).start()

    def quarter(slot, dist):
        rows = pl.ds(pl.multiple_of(((x - dist + NX) % NX) * QUARTER, 16), QUARTER)
        return wbuf.at[pl.ds(slot, HALF), rows, :]

    mine = 1 + HALF * core
    other = 1 + HALF * (1 - core)

    def copy_p2(dist):
        return copy(quarter(mine, 0), quarter(mine, 0), p2_s.at[dist], p2_r.at[dist], at_x(dist), m)

    def arrival_p2(dist):
        return copy(quarter(mine, dist), quarter(mine, dist), p2_s.at[dist], p2_r.at[dist], at_x(-dist), m)

    def copy_sib(dist, slot):
        return copy(quarter(slot, dist), quarter(slot, dist), p3_s.at[dist], p3_r.at[dist], sibling, m)

    for j in range(HALF):
        copy_p1(j).wait_recv()
    for dist in range(1, NX):
        copy_p2(dist).start()
    copy_sib(0, mine).start()

    for hop in range(1, HALF):
        for b in order:
            send_right(b, hop - 1).wait_recv()
            if hop + 1 < HALF or b < NB // 2:
                send_right(b, hop).start()
            send_left(b, hop - 1).wait_recv()
            if hop + 1 < HALF or b >= NB // 2:
                send_left(b, hop).start()
        if hop == 3:
            for dist in range(1, NX):
                arrival_p2(dist).wait_recv()
                copy_sib(dist, mine).start()
    for dist in range(NX):
        copy_sib(dist, other).wait_recv()

    def copy_y(b):
        return copy(psend.at[b], precv.at[b], y_s.at[b], y_r.at[b], s, partner)

    theirs_at = pl.multiple_of((1 - yl) * MINE, 16)
    mine_at = pl.multiple_of(yl * MINE, 16)

    def product(b, slots, at):
        rows = jnp.concatenate([wbuf[i, pl.ds(at, MINE), :] for i in slots], axis=1)
        heads = jnp.concatenate([ho[b, i] for i in slots], axis=1)
        return lax.dot_general(rows, heads, NT, preferred_element_type=F32)

    early = [i for i in range(NZ) if i != HALF]
    for b in order:
        theirs = product(b, early, theirs_at)
        mine_part = product(b, early, mine_at)
        if b < NB // 2:
            send_right(b, HALF - 1).wait_recv()
        else:
            send_left(b, HALF - 1).wait_recv()
        psend[b] = (theirs + product(b, [HALF], theirs_at)).astype(BF)
        copy_y(b).start()
        own[b] = mine_part + product(b, [HALF], mine_at)
    for b in order:
        copy_y(b).wait_recv()
        out_ref[:, b * BLK : (b + 1) * BLK] = (own[b] + precv[b].astype(F32)).astype(BF)

    @pl.when(straight)
    def _():
        for j in order:
            copy_a(j).wait_send()

    @pl.when(around)
    def _():
        for j in order:
            copy_in(j).wait_send()

    @pl.when(passes)
    def _():
        for j in order:
            copy_on(j).wait_send()

    @pl.when(core == 0)
    def _():
        copy_c1().wait_send()

    @pl.when(has_prev)
    def _():
        for j in order:
            copy_b(j, yl).wait_send()

    @pl.when(has_prev & (core == 1))
    def _():
        for j in order:
            copy_c2(j, yl).wait_send()
            copy_c2(j, 1 - yl).wait_send()

    for j in range(HALF):
        copy_p1(j).wait_send()
    for dist in range(1, NX):
        copy_p2(dist).wait_send()
    for dist in range(NX):
        copy_sib(dist, mine).wait_send()
    for b in order:
        for hop in range(HALF):
            if hop + 1 < HALF or b < NB // 2:
                send_right(b, hop).wait_send()
            if hop + 1 < HALF or b >= NB // 2:
                send_left(b, hop).wait_send()
        copy_y(b).wait_send()


def per_device(hidden_in, norm_gain, query_weight, kv_weight, out_weight):
    index = np.arange(HD) % (HD // 2)
    freq = np.exp(-math.log(10000.0) * index * (2.0 / HD)).astype(np.float32)[None, :]
    any_space = pl.BlockSpec(memory_space=pl.ANY)
    vmem = pl.BlockSpec(memory_space=pltpu.VMEM)
    dma = pltpu.SemaphoreType.DMA
    return pl.pallas_call(
        kernel,
        out_shape=jax.ShapeDtypeStruct((MINE, ROWS), BF),
        in_specs=[any_space, vmem, any_space, any_space, any_space, vmem],
        out_specs=vmem,
        scratch_shapes=[
            pltpu.VMEM((NK, ROWS, KC), BF),
            pltpu.VMEM((NK, ROWS, KC), BF),
            pltpu.VMEM((D, HD), BF),
            pltpu.VMEM((NK, KC, 2 * HD), BF),
            pltpu.VMEM((HD, D), BF),
            pltpu.VMEM((D, HD), BF),
            pltpu.VMEM((NZ + 1, FEATS, HD), BF),
            pltpu.VMEM((2, 3 * ROWS, HD), BF),
            pltpu.VMEM((ROWS, HD), BF),
            pltpu.VMEM((NB, NZ, BLK, HD), BF),
            pltpu.VMEM((ROWS, 2 * HD), F32),
            pltpu.VMEM((ROWS, HD), F32),
            pltpu.VMEM((ROWS, HD), F32),
            pltpu.VMEM((ROWS, HD), F32),
            pltpu.VMEM((NB, MINE, BLK), BF),
            pltpu.VMEM((NB, MINE, BLK), BF),
            pltpu.VMEM((NB, MINE, BLK), F32),
            pltpu.VMEM((NB, BLK, HD), BF),
            dma((NK,)), dma((NK,)), dma, dma,
            dma((NB,)), dma((NB,)), dma((NB,)), dma((NB,)),
            dma((1,)), dma((1,)), dma((2, NB)), dma((2, NB)),
            dma((HALF,)), dma((HALF,)), dma((NX,)), dma((NX,)), dma((NX,)), dma((NX,)),
            dma((NB, HALF)), dma((NB, HALF)), dma((NB, NZ)), dma((NB,)), dma((NB,)),
            dma((2, NB)), dma((NB,)),
        ],
        compiler_params=pltpu.CompilerParams(
            collective_id=0, has_side_effects=True, vmem_limit_bytes=60 * 1024 * 1024
        ),
    )(
        hidden_in, norm_gain, query_weight, kv_weight, out_weight, jnp.asarray(freq),
    )


def solution(mesh):
    in_specs = (P("seq", None), P(), P(None, "mp"), P(None, "mp"), P("mp", None))
    out_specs = P("mp", "seq")
    return jax.shard_map(
        per_device, mesh=mesh, in_specs=in_specs, out_specs=out_specs, check_vma=False
    )
```

```python
import math

import jax
import jax.numpy as jnp
import numpy as np
from jax import lax
from jax.experimental import pallas as pl
from jax.experimental.pallas import tpu as pltpu
from jax.sharding import PartitionSpec as P

MESH = pl.DeviceIdType.MESH
BF = jnp.bfloat16
F32 = jnp.float32

D = 5376
HD = 128
WINDOW = 1024
ROWS = 512
NZ = 12
NX = 4
HALF = NZ // 2
FEATS = D // NZ
MINE = FEATS // 2
QUARTER = FEATS // NX
NK = 7
KC = D // NK
AHEAD = 4
NB = 4
BLK = ROWS // NB
KEYS = WINDOW + BLK
SCALE = math.log2(math.e) / math.sqrt(168.0)

NT = (((1,), (1,)), ((), ()))


def kernel(
    x_hbm, gain_ref, wq_hbm, wkv_hbm, wo_hbm, freq_ref, out_ref,
    xb, xg, wqb, wkvb, wob, wt, wbuf, kv, qb, ho, acc, ss, rc, rs, psend, precv, own, rel,
    ld_x, ld_kv, ld_q, ld_o,
    a_s, a_r, b_s, b_r, c1_s, c1_r, c2_s, c2_r,
    p1_s, p1_r, p2_s, p2_r, p3_s, p3_r,
    r_s, l_s, g_r, y_s, y_r, f_s, f_r,
):
    s = lax.axis_index("seq")
    m = lax.axis_index("mp")
    nseq = lax.axis_size("seq")
    z = m // 2
    yl = m % 2
    core = s % 2
    x = (s // 2) % NX
    partner = m + 1 - 2 * yl
    sibling = s + 1 - 2 * core
    has_prev = s >= 2
    has_next = s < nseq - 2
    turns = x == NX - 1
    passes = (x == 0) & (s < nseq - 2 * NX) & (yl == 1)
    passed = (x == 0) & has_prev & (yl == 0)

    def at_z(dist):
        return ((z + dist + NZ) % NZ) * 2 + yl

    def at_x(dist):
        return s + 2 * ((x + dist) % NX - x)

    def copy(src, dst, ssem, rsem, seq, mp):
        return pltpu.make_async_remote_copy(
            src_ref=src, dst_ref=dst, send_sem=ssem, recv_sem=rsem,
            device_id=(seq, mp), device_id_type=MESH,
        )

    load_o = pltpu.make_async_copy(wo_hbm, wob, ld_o)
    load_q = pltpu.make_async_copy(wq_hbm, wqb, ld_q)

    def load_x(k):
        return pltpu.make_async_copy(x_hbm.at[:, pl.ds(k * KC, KC)], xb.at[k], ld_x.at[k])

    def load_kv(k):
        return pltpu.make_async_copy(wkv_hbm.at[pl.ds(k * KC, KC), :], wkvb.at[k], ld_kv.at[k])

    def load(k):
        if k < NK:
            load_x(k).start()
            load_kv(k).start()
        elif k == NK:
            load_o.start()
        elif k == NK + 1:
            load_q.start()

    for k in range(AHEAD):
        load(k)

    barrier = pltpu.get_barrier_semaphore()

    def greet(seq, mp):
        pl.semaphore_signal(barrier, inc=1, device_id=(seq, mp), device_id_type=MESH)

    for dist in range(1, NZ):
        greet(s, at_z(dist))
    for dist in range(1, NX):
        greet(at_x(dist), m)
    greet(sibling, m)
    greet(s, partner)

    @pl.when(has_prev)
    def _():
        greet(s - 2, m)

    @pl.when(has_next)
    def _():
        greet(s + 2, m)

    @pl.when(passes)
    def _():
        greet(s + 2 * NX, m - 1)

    @pl.when(passed)
    def _():
        greet(s - 2 * NX, m + 1)

    lane = lax.broadcasted_iota(jnp.int32, (32, HD), 1)
    sign = jnp.where(lane < HD // 2, -1.0, 1.0).astype(F32)
    row = lax.broadcasted_iota(jnp.int32, (48, HD), 0)
    place = jnp.where(row < 16, ROWS * s + 32 * row, row - 16).astype(F32)
    angle = place * freq_ref[...]
    cosine = jnp.cos(angle)
    sine = jnp.sin(angle)
    cos_low = cosine[16:48, :]
    sin_low = sine[16:48, :]
    for a in range(16):
        cos_high = cosine[a : a + 1, :]
        sin_high = sine[a : a + 1, :]
        rc[32 * a : 32 * a + 32, :] = cos_high * cos_low - sin_high * sin_low
        rs[32 * a : 32 * a + 32, :] = (sin_high * cos_low + cos_high * sin_low) * sign

    @pl.when(s == 0)
    def _():
        kv[:, 0 : 2 * ROWS, :] = jnp.zeros((2, 2 * ROWS, HD), BF)

    @pl.when(s == 1)
    def _():
        kv[:, 0:ROWS, :] = jnp.zeros((2, ROWS, HD), BF)

    def scale(k):
        gain = gain_ref[pl.ds(k * KC, KC)].reshape(1, KC)
        for r in range(0, ROWS, 16):
            wide = xb[k, r : r + 16, :].astype(F32)
            square = wide * wide
            part = square[:, 0:HD]
            for c in range(HD, KC, HD):
                part = part + square[:, c : c + HD]
            if k == 0:
                ss[r : r + 16, :] = part
            else:
                ss[r : r + 16, :] += part
            xg[k, r : r + 16, :] = (wide * gain).astype(BF)

    def arrive(k):
        load_x(k).wait()
        load_kv(k).wait()
        load(k + AHEAD)

    arrive(0)
    scale(0)
    for k in range(NK):
        if k + 1 < NK:
            arrive(k + 1)
            scale(k + 1)
        part = jnp.dot(xg[k], wkvb[k], preferred_element_type=F32)
        if k == 0:
            acc[...] = part
        else:
            acc[...] += part
    inverse = lax.rsqrt(jnp.sum(ss[...], axis=1, keepdims=True) * (1.0 / D) + 1e-06)

    def rope(t):
        return t * rc[...] + pltpu.roll(t, HD // 2, 1) * rs[...]

    kv[0, 2 * ROWS : 3 * ROWS, :] = rope(acc[:, 0:HD] * inverse).astype(BF)
    kv[1, 2 * ROWS : 3 * ROWS, :] = (acc[:, HD : 2 * HD] * inverse).astype(BF)

    pl.semaphore_wait(
        barrier,
        (NZ - 1) + (NX - 1) + 2 + has_prev.astype(jnp.int32) + has_next.astype(jnp.int32)
        + passes.astype(jnp.int32) + passed.astype(jnp.int32),
    )

    def copy_a(j):
        return copy(
            kv.at[yl, pl.ds(2 * ROWS + j * BLK, BLK), :], kv.at[yl, pl.ds(j * BLK, BLK), :],
            a_s.at[j], a_r.at[j], s + 2, m,
        )

    def copy_b(j, half):
        block = kv.at[half, pl.ds(j * BLK, BLK), :]
        return copy(block, block, b_s.at[j], b_r.at[j], s, partner)

    def copy_c1():
        return copy(
            kv.at[:, pl.ds(2 * ROWS, ROWS), :], kv.at[:, pl.ds(ROWS, ROWS), :],
            c1_s.at[0], c1_r.at[0], sibling, m,
        )

    def copy_c2(j, half):
        return copy(
            kv.at[half, pl.ds(j * BLK, BLK), :], kv.at[half, pl.ds(ROWS + j * BLK, BLK), :],
            c2_s.at[half, j], c2_r.at[half, j], sibling, m,
        )

    order = tuple(range(NB - 1, -1, -1))

    def copy_in(j):
        return copy(
            kv.at[0, pl.ds(2 * ROWS + j * BLK, BLK), :], rel.at[j], f_s.at[0, j], f_r.at[j], at_x(1), m,
        )

    def copy_on(j):
        return copy(
            rel.at[j], kv.at[0, pl.ds(j * BLK, BLK), :], f_s.at[1, j], a_r.at[j], s + 2 * NX, m - 1,
        )

    straight = has_next & (jnp.logical_not(turns) | (yl == 1))
    around = has_next & turns & (yl == 1)

    def send_on(which):
        @pl.when(straight)
        def _():
            for j in which:
                copy_a(j).start()

        @pl.when(around)
        def _():
            for j in which:
                copy_in(j).start()

    @pl.when(core == 1)
    def _():
        send_on(order)

    @pl.when(core == 0)
    def _():
        send_on(order[:1])
        copy_c1().start()

    load_o.wait()
    for f in range(D // HD):
        wt[f * HD : (f + 1) * HD, :] = wob[:, f * HD : (f + 1) * HD].T

    def copy_p1(j):
        dist = (j + 1) * (1 - 2 * core)
        plane = (z + dist + NZ) % NZ
        slot = 1 + j + HALF * core
        return copy(
            wt.at[pl.ds(pl.multiple_of(plane * FEATS + x * QUARTER, 16), QUARTER), :],
            wbuf.at[slot, pl.ds(pl.multiple_of(x * QUARTER, 16), QUARTER), :],
            p1_s.at[j], p1_r.at[j], s, plane * 2 + yl,
        )

    for j in range(HALF):
        copy_p1(j).start()
    wbuf[0] = wt[pl.ds(pl.multiple_of(z * FEATS, 16), FEATS), :]

    load_q.wait()
    queries = jnp.dot(xg[0], wqb[0:KC, :], preferred_element_type=F32)
    for k in range(1, NK):
        queries = queries + jnp.dot(
            xg[k], wqb[k * KC : (k + 1) * KC, :], preferred_element_type=F32
        )
    qb[...] = (rope(queries * inverse) * SCALE).astype(BF)

    @pl.when(core == 0)
    def _():
        send_on(order[1:])

    def quarter(slot, dist):
        rows = pl.ds(pl.multiple_of(((x - dist + NX) % NX) * QUARTER, 16), QUARTER)
        return wbuf.at[pl.ds(slot, HALF), rows, :]

    mine = 1 + HALF * core
    other = 1 + HALF * (1 - core)

    def copy_p2(dist):
        return copy(quarter(mine, 0), quarter(mine, 0), p2_s.at[dist], p2_r.at[dist], at_x(dist), m)

    def arrival_p2(dist):
        return copy(quarter(mine, dist), quarter(mine, dist), p2_s.at[dist], p2_r.at[dist], at_x(-dist), m)

    def copy_sib(dist, slot):
        return copy(quarter(slot, dist), quarter(slot, dist), p3_s.at[dist], p3_r.at[dist], sibling, m)

    def spread():
        for j in range(HALF):
            copy_p1(j).wait_recv()
        for dist in (2, 1, 3):
            copy_p2(dist).start()
        copy_sib(0, mine).start()

    late = has_prev & (x == 0)

    @pl.when(passes)
    def _():
        for j in order:
            copy_in(j).wait_recv()
            copy_on(j).start()

    @pl.when(has_prev & (core == 1))
    def _():
        for j in order:
            copy_a(j).wait_recv()
            copy_b(j, yl).start()
            copy_c2(j, yl).start()

        @pl.when(late)
        def _():
            spread()

        for j in order:
            copy_b(j, 1 - yl).wait_recv()
            copy_c2(j, 1 - yl).start()

    @pl.when(has_prev & (core == 0))
    def _():
        for j in order:
            copy_a(j).wait_recv()
            copy_b(j, yl).start()

        @pl.when(late)
        def _():
            spread()

        for j in order:
            copy_c2(j, yl).wait_recv()
            copy_c2(j, 1 - yl).wait_recv()

    @pl.when(core == 1)
    def _():
        copy_c1().wait_recv()

    right, left = at_z(1), at_z(-1)

    def send_right(b, d):
        return copy(ho.at[b, d], ho.at[b, d + 1], r_s.at[b, d], g_r.at[b, d + 1], s, right)

    def send_left(b, e):
        to = HALF if e == HALF - 1 else HALF + e + 1
        frm = 0 if e == 0 else HALF + e
        return copy(ho.at[b, frm], ho.at[b, to], l_s.at[b, e], g_r.at[b, to], s, left)

    first_key = jnp.maximum(WINDOW - ROWS * s, 0)
    query_row = lax.broadcasted_iota(jnp.int32, (BLK, BLK), 0)
    key_row = lax.broadcasted_iota(jnp.int32, (BLK, BLK), 1)
    column = lax.broadcasted_iota(jnp.int32, (1, KEYS), 1)
    for b in order:
        start = b * BLK

        @pl.when(has_prev & (core == 0))
        def _():
            copy_b(b, 1 - yl).wait_recv()

        scores = lax.dot_general(
            qb[start : start + BLK, :], kv[0, start : start + KEYS, :], NT,
            preferred_element_type=F32,
        )
        exists = column + start >= first_key
        scores = jnp.where(exists, scores, -1e30)
        scores = jnp.concatenate(
            [
                jnp.where(key_row > query_row, scores[:, 0:BLK], -1e30),
                scores[:, BLK:WINDOW],
                jnp.where(key_row <= query_row, scores[:, WINDOW:KEYS], -1e30),
            ],
            axis=1,
        )
        weights = jnp.exp2(scores - jnp.max(scores, axis=1, keepdims=True))
        total = jnp.sum(weights, axis=1, keepdims=True)
        mixed = jnp.dot(
            weights.astype(BF), kv[1, start : start + KEYS, :], preferred_element_type=F32
        )
        ho[b, 0] = (mixed / total).astype(BF)
        send_right(b, 0).start()
        send_left(b, 0).start()

    @pl.when(jnp.logical_not(late))
    def _():
        spread()

    for hop in range(1, HALF):
        for b in order:
            send_right(b, hop - 1).wait_recv()
            if hop + 1 < HALF or b < NB // 2:
                send_right(b, hop).start()
            send_left(b, hop - 1).wait_recv()
            if hop + 1 < HALF or b >= NB // 2:
                send_left(b, hop).start()
    for dist in range(1, NX):
        arrival_p2(dist).wait_recv()
        copy_sib(dist, mine).start()
    for dist in range(NX):
        copy_sib(dist, other).wait_recv()

    def copy_y(b):
        return copy(psend.at[b], precv.at[b], y_s.at[b], y_r.at[b], s, partner)

    theirs_at = pl.multiple_of((1 - yl) * MINE, 16)
    mine_at = pl.multiple_of(yl * MINE, 16)

    def product(b, slots, at):
        rows = jnp.concatenate([wbuf[i, pl.ds(at, MINE), :] for i in slots], axis=1)
        heads = jnp.concatenate([ho[b, i] for i in slots], axis=1)
        return lax.dot_general(rows, heads, NT, preferred_element_type=F32)

    early = [i for i in range(NZ) if i != HALF]
    for b in order:
        theirs = product(b, early, theirs_at)
        mine_part = product(b, early, mine_at)
        if b < NB // 2:
            send_right(b, HALF - 1).wait_recv()
        else:
            send_left(b, HALF - 1).wait_recv()
        psend[b] = (theirs + product(b, [HALF], theirs_at)).astype(BF)
        copy_y(b).start()
        own[b] = mine_part + product(b, [HALF], mine_at)
    for b in order:
        copy_y(b).wait_recv()
        out_ref[:, b * BLK : (b + 1) * BLK] = (own[b] + precv[b].astype(F32)).astype(BF)

    @pl.when(straight)
    def _():
        for j in order:
            copy_a(j).wait_send()

    @pl.when(around)
    def _():
        for j in order:
            copy_in(j).wait_send()

    @pl.when(passes)
    def _():
        for j in order:
            copy_on(j).wait_send()

    @pl.when(core == 0)
    def _():
        copy_c1().wait_send()

    @pl.when(has_prev)
    def _():
        for j in order:
            copy_b(j, yl).wait_send()

    @pl.when(has_prev & (core == 1))
    def _():
        for j in order:
            copy_c2(j, yl).wait_send()
            copy_c2(j, 1 - yl).wait_send()

    for j in range(HALF):
        copy_p1(j).wait_send()
    for dist in range(1, NX):
        copy_p2(dist).wait_send()
    for dist in range(NX):
        copy_sib(dist, mine).wait_send()
    for b in order:
        for hop in range(HALF):
            if hop + 1 < HALF or b < NB // 2:
                send_right(b, hop).wait_send()
            if hop + 1 < HALF or b >= NB // 2:
                send_left(b, hop).wait_send()
        copy_y(b).wait_send()


def per_device(hidden_in, norm_gain, query_weight, kv_weight, out_weight):
    index = np.arange(HD) % (HD // 2)
    freq = np.exp(-math.log(10000.0) * index * (2.0 / HD)).astype(np.float32)[None, :]
    any_space = pl.BlockSpec(memory_space=pl.ANY)
    vmem = pl.BlockSpec(memory_space=pltpu.VMEM)
    dma = pltpu.SemaphoreType.DMA
    return pl.pallas_call(
        kernel,
        out_shape=jax.ShapeDtypeStruct((MINE, ROWS), BF),
        in_specs=[any_space, vmem, any_space, any_space, any_space, vmem],
        out_specs=vmem,
        scratch_shapes=[
            pltpu.VMEM((NK, ROWS, KC), BF),
            pltpu.VMEM((NK, ROWS, KC), BF),
            pltpu.VMEM((D, HD), BF),
            pltpu.VMEM((NK, KC, 2 * HD), BF),
            pltpu.VMEM((HD, D), BF),
            pltpu.VMEM((D, HD), BF),
            pltpu.VMEM((NZ + 1, FEATS, HD), BF),
            pltpu.VMEM((2, 3 * ROWS, HD), BF),
            pltpu.VMEM((ROWS, HD), BF),
            pltpu.VMEM((NB, NZ, BLK, HD), BF),
            pltpu.VMEM((ROWS, 2 * HD), F32),
            pltpu.VMEM((ROWS, HD), F32),
            pltpu.VMEM((ROWS, HD), F32),
            pltpu.VMEM((ROWS, HD), F32),
            pltpu.VMEM((NB, MINE, BLK), BF),
            pltpu.VMEM((NB, MINE, BLK), BF),
            pltpu.VMEM((NB, MINE, BLK), F32),
            pltpu.VMEM((NB, BLK, HD), BF),
            dma((NK,)), dma((NK,)), dma, dma,
            dma((NB,)), dma((NB,)), dma((NB,)), dma((NB,)),
            dma((1,)), dma((1,)), dma((2, NB)), dma((2, NB)),
            dma((HALF,)), dma((HALF,)), dma((NX,)), dma((NX,)), dma((NX,)), dma((NX,)),
            dma((NB, HALF)), dma((NB, HALF)), dma((NB, NZ)), dma((NB,)), dma((NB,)),
            dma((2, NB)), dma((NB,)),
        ],
        compiler_params=pltpu.CompilerParams(
            collective_id=0, has_side_effects=True, vmem_limit_bytes=60 * 1024 * 1024
        ),
    )(
        hidden_in, norm_gain, query_weight, kv_weight, out_weight, jnp.asarray(freq),
    )


def solution(mesh):
    in_specs = (P("seq", None), P(), P(None, "mp"), P(None, "mp"), P("mp", None))
    out_specs = P("mp", "seq")
    return jax.shard_map(
        per_device, mesh=mesh, in_specs=in_specs, out_specs=out_specs, check_vma=False
    )
```

```python
import math

import jax
import jax.numpy as jnp
import numpy as np
from jax import lax
from jax.experimental import pallas as pl
from jax.experimental.pallas import tpu as pltpu
from jax.sharding import PartitionSpec as P

MESH = pl.DeviceIdType.MESH
BF = jnp.bfloat16
F32 = jnp.float32

D = 5376
HD = 128
WINDOW = 1024
ROWS = 512
NZ = 12
NX = 4
HALF = NZ // 2
FEATS = D // NZ
MINE = FEATS // 2
QUARTER = FEATS // NX
NK = 7
KC = D // NK
AHEAD = 4
NB = 4
BLK = ROWS // NB
KEYS = WINDOW + BLK
SCALE = math.log2(math.e) / math.sqrt(168.0)

NT = (((1,), (1,)), ((), ()))


def kernel(
    x_hbm, gain_ref, wq_hbm, wkv_hbm, wo_hbm, freq_ref, out_ref,
    xb, xg, wqb, wkvb, wob, wt, wbuf, kv, qb, ho, acc, ss, rc, rs, psend, precv, own, rel, h2,
    ld_x, ld_kv, ld_q, ld_o,
    a_s, a_r, b_s, b_r, c1_s, c1_r, c2_s, c2_r,
    p1_s, p1_r, p2_s, p2_r, p3_s, p3_r,
    r_s, l_s, g_r, y_s, y_r, f_s, f_r,
    r2_s, l2_s, g2_r, d_s,
):
    s = lax.axis_index("seq")
    m = lax.axis_index("mp")
    nseq = lax.axis_size("seq")
    z = m // 2
    yl = m % 2
    core = s % 2
    x = (s // 2) % NX
    partner = m + 1 - 2 * yl
    sibling = s + 1 - 2 * core
    has_prev = s >= 2
    has_next = s < nseq - 2
    turns = x == NX - 1
    passes = (x == 0) & (s < nseq - 2 * NX) & (yl == 1)
    passed = (x == 0) & has_prev & (yl == 0)

    def at_z(dist):
        return ((z + dist + NZ) % NZ) * 2 + yl

    def at_x(dist):
        return s + 2 * ((x + dist) % NX - x)

    def copy(src, dst, ssem, rsem, seq, mp):
        return pltpu.make_async_remote_copy(
            src_ref=src, dst_ref=dst, send_sem=ssem, recv_sem=rsem,
            device_id=(seq, mp), device_id_type=MESH,
        )

    load_o = pltpu.make_async_copy(wo_hbm, wob, ld_o)
    load_q = pltpu.make_async_copy(wq_hbm, wqb, ld_q)

    def load_x(k):
        return pltpu.make_async_copy(x_hbm.at[:, pl.ds(k * KC, KC)], xb.at[k], ld_x.at[k])

    def load_kv(k):
        return pltpu.make_async_copy(wkv_hbm.at[pl.ds(k * KC, KC), :], wkvb.at[k], ld_kv.at[k])

    def load(k):
        if k < NK:
            load_x(k).start()
            load_kv(k).start()
        elif k == NK:
            load_o.start()
        elif k == NK + 1:
            load_q.start()

    for k in range(AHEAD):
        load(k)

    barrier = pltpu.get_barrier_semaphore()

    def greet(seq, mp):
        pl.semaphore_signal(barrier, inc=1, device_id=(seq, mp), device_id_type=MESH)

    for dist in range(1, NZ):
        greet(s, at_z(dist))
    for dist in range(1, NX):
        greet(at_x(dist), m)
    greet(sibling, m)
    greet(sibling, at_z(1))
    greet(sibling, at_z(-1))
    greet(s, partner)

    @pl.when(has_prev)
    def _():
        greet(s - 2, m)

    @pl.when(has_next)
    def _():
        greet(s + 2, m)

    @pl.when(passes)
    def _():
        greet(s + 2 * NX, m - 1)

    @pl.when(passed)
    def _():
        greet(s - 2 * NX, m + 1)

    lane = lax.broadcasted_iota(jnp.int32, (32, HD), 1)
    sign = jnp.where(lane < HD // 2, -1.0, 1.0).astype(F32)
    row = lax.broadcasted_iota(jnp.int32, (48, HD), 0)
    place = jnp.where(row < 16, ROWS * s + 32 * row, row - 16).astype(F32)
    angle = place * freq_ref[...]
    cosine = jnp.cos(angle)
    sine = jnp.sin(angle)
    cos_low = cosine[16:48, :]
    sin_low = sine[16:48, :]
    for a in range(16):
        cos_high = cosine[a : a + 1, :]
        sin_high = sine[a : a + 1, :]
        rc[32 * a : 32 * a + 32, :] = cos_high * cos_low - sin_high * sin_low
        rs[32 * a : 32 * a + 32, :] = (sin_high * cos_low + cos_high * sin_low) * sign

    @pl.when(s == 0)
    def _():
        kv[:, 0 : 2 * ROWS, :] = jnp.zeros((2, 2 * ROWS, HD), BF)

    @pl.when(s == 1)
    def _():
        kv[:, 0:ROWS, :] = jnp.zeros((2, ROWS, HD), BF)

    def scale(k):
        gain = gain_ref[pl.ds(k * KC, KC)].reshape(1, KC)
        for r in range(0, ROWS, 16):
            wide = xb[k, r : r + 16, :].astype(F32)
            square = wide * wide
            part = square[:, 0:HD]
            for c in range(HD, KC, HD):
                part = part + square[:, c : c + HD]
            if k == 0:
                ss[r : r + 16, :] = part
            else:
                ss[r : r + 16, :] += part
            xg[k, r : r + 16, :] = (wide * gain).astype(BF)

    def arrive(k):
        load_x(k).wait()
        load_kv(k).wait()
        load(k + AHEAD)

    arrive(0)
    scale(0)
    for k in range(NK):
        if k + 1 < NK:
            arrive(k + 1)
            scale(k + 1)
        part = jnp.dot(xg[k], wkvb[k], preferred_element_type=F32)
        if k == 0:
            acc[...] = part
        else:
            acc[...] += part
    inverse = lax.rsqrt(jnp.sum(ss[...], axis=1, keepdims=True) * (1.0 / D) + 1e-06)

    def rope(t):
        return t * rc[...] + pltpu.roll(t, HD // 2, 1) * rs[...]

    kv[0, 2 * ROWS : 3 * ROWS, :] = rope(acc[:, 0:HD] * inverse).astype(BF)
    kv[1, 2 * ROWS : 3 * ROWS, :] = (acc[:, HD : 2 * HD] * inverse).astype(BF)

    pl.semaphore_wait(
        barrier,
        (NZ - 1) + (NX - 1) + 4 + has_prev.astype(jnp.int32) + has_next.astype(jnp.int32)
        + passes.astype(jnp.int32) + passed.astype(jnp.int32),
    )

    def copy_a(j):
        return copy(
            kv.at[yl, pl.ds(2 * ROWS + j * BLK, BLK), :], kv.at[yl, pl.ds(j * BLK, BLK), :],
            a_s.at[j], a_r.at[j], s + 2, m,
        )

    def copy_b(j, half):
        block = kv.at[half, pl.ds(j * BLK, BLK), :]
        return copy(block, block, b_s.at[j], b_r.at[j], s, partner)

    def copy_c1():
        return copy(
            kv.at[:, pl.ds(2 * ROWS, ROWS), :], kv.at[:, pl.ds(ROWS, ROWS), :],
            c1_s.at[0], c1_r.at[0], sibling, m,
        )

    def copy_c2(j, half):
        return copy(
            kv.at[half, pl.ds(j * BLK, BLK), :], kv.at[half, pl.ds(ROWS + j * BLK, BLK), :],
            c2_s.at[half, j], c2_r.at[half, j], sibling, m,
        )

    order = tuple(range(NB - 1, -1, -1))

    def copy_in(j):
        return copy(
            kv.at[0, pl.ds(2 * ROWS + j * BLK, BLK), :], rel.at[j], f_s.at[0, j], f_r.at[j], at_x(1), m,
        )

    def copy_on(j):
        return copy(
            rel.at[j], kv.at[0, pl.ds(j * BLK, BLK), :], f_s.at[1, j], a_r.at[j], s + 2 * NX, m - 1,
        )

    straight = has_next & (jnp.logical_not(turns) | (yl == 1))
    around = has_next & turns & (yl == 1)

    def send_on(which):
        @pl.when(straight)
        def _():
            for j in which:
                copy_a(j).start()

        @pl.when(around)
        def _():
            for j in which:
                copy_in(j).start()

    @pl.when(core == 1)
    def _():
        send_on(order)

    @pl.when(core == 0)
    def _():
        send_on(order[:1])
        copy_c1().start()

    load_o.wait()
    for f in range(D // HD):
        wt[f * HD : (f + 1) * HD, :] = wob[:, f * HD : (f + 1) * HD].T

    def copy_p1(j):
        dist = (j + 1) * (1 - 2 * core)
        plane = (z + dist + NZ) % NZ
        slot = 1 + j + HALF * core
        return copy(
            wt.at[pl.ds(pl.multiple_of(plane * FEATS + x * QUARTER, 16), QUARTER), :],
            wbuf.at[slot, pl.ds(pl.multiple_of(x * QUARTER, 16), QUARTER), :],
            p1_s.at[j], p1_r.at[j], s, plane * 2 + yl,
        )

    for j in range(HALF):
        copy_p1(j).start()
    wbuf[0] = wt[pl.ds(pl.multiple_of(z * FEATS, 16), FEATS), :]

    load_q.wait()
    queries = jnp.dot(xg[0], wqb[0:KC, :], preferred_element_type=F32)
    for k in range(1, NK):
        queries = queries + jnp.dot(
            xg[k], wqb[k * KC : (k + 1) * KC, :], preferred_element_type=F32
        )
    qb[...] = (rope(queries * inverse) * SCALE).astype(BF)

    @pl.when(core == 0)
    def _():
        send_on(order[1:])

    def quarter(slot, dist):
        rows = pl.ds(pl.multiple_of(((x - dist + NX) % NX) * QUARTER, 16), QUARTER)
        return wbuf.at[pl.ds(slot, HALF), rows, :]

    mine = 1 + HALF * core
    other = 1 + HALF * (1 - core)

    def copy_p2(dist):
        return copy(quarter(mine, 0), quarter(mine, 0), p2_s.at[dist], p2_r.at[dist], at_x(dist), m)

    def arrival_p2(dist):
        return copy(quarter(mine, dist), quarter(mine, dist), p2_s.at[dist], p2_r.at[dist], at_x(-dist), m)

    def copy_sib(dist, slot):
        return copy(quarter(slot, dist), quarter(slot, dist), p3_s.at[dist], p3_r.at[dist], sibling, m)

    def spread():
        for j in range(HALF):
            copy_p1(j).wait_recv()
        for dist in (2, 1, 3):
            copy_p2(dist).start()
        copy_sib(0, mine).start()

    late = has_prev & (x == 0)

    @pl.when(passes)
    def _():
        for j in order:
            copy_in(j).wait_recv()
            copy_on(j).start()

    @pl.when(has_prev & (core == 1))
    def _():
        for j in order:
            copy_a(j).wait_recv()
            copy_b(j, yl).start()
            copy_c2(j, yl).start()

        @pl.when(late)
        def _():
            spread()

        for j in order:
            copy_b(j, 1 - yl).wait_recv()
            copy_c2(j, 1 - yl).start()

    @pl.when(has_prev & (core == 0))
    def _():
        for j in order:
            copy_a(j).wait_recv()
            copy_b(j, yl).start()

        @pl.when(late)
        def _():
            spread()

        for j in order:
            copy_c2(j, yl).wait_recv()
            copy_c2(j, 1 - yl).wait_recv()

    @pl.when(core == 1)
    def _():
        copy_c1().wait_recv()

    right, left = at_z(1), at_z(-1)

    def send_right(b, d):
        return copy(ho.at[b, d], ho.at[b, d + 1], r_s.at[b, d], g_r.at[b, d + 1], s, right)

    def send_left(b, e):
        to = HALF if e == HALF - 1 else HALF + e + 1
        frm = 0 if e == 0 else HALF + e
        return copy(ho.at[b, frm], ho.at[b, to], l_s.at[b, e], g_r.at[b, to], s, left)

    def send_right2(b, d):
        return copy(h2.at[b, d], h2.at[b, d + 1], r2_s.at[b, d], g2_r.at[b, d + 1], s, right)

    def send_left2(b, e):
        to = HALF if e == HALF - 1 else HALF + e + 1
        return copy(h2.at[b, HALF + e], h2.at[b, to], l2_s.at[b, e], g2_r.at[b, to], s, left)

    def enter_right(b):
        return copy(ho.at[b, 0], h2.at[b, 1], r2_s.at[b, 0], g2_r.at[b, 1], sibling, right)

    def enter_left(b):
        return copy(ho.at[b, 0], h2.at[b, HALF + 1], l2_s.at[b, 0], g2_r.at[b, HALF + 1], sibling, left)

    def hand(b, i):
        return copy(h2.at[b, i], ho.at[b, i], d_s.at[b, i], g_r.at[b, i], sibling, m)

    def goes_right(b, hop):
        return hop + 1 < HALF or b < NB // 2

    def goes_left(b, hop):
        return hop + 1 < HALF or b >= NB // 2

    first_key = jnp.maximum(WINDOW - ROWS * s, 0)
    query_row = lax.broadcasted_iota(jnp.int32, (BLK, BLK), 0)
    key_row = lax.broadcasted_iota(jnp.int32, (BLK, BLK), 1)
    column = lax.broadcasted_iota(jnp.int32, (1, KEYS), 1)
    for b in order:
        start = b * BLK

        @pl.when(has_prev & (core == 0))
        def _():
            copy_b(b, 1 - yl).wait_recv()

        scores = lax.dot_general(
            qb[start : start + BLK, :], kv[0, start : start + KEYS, :], NT,
            preferred_element_type=F32,
        )
        exists = column + start >= first_key
        scores = jnp.where(exists, scores, -1e30)
        scores = jnp.concatenate(
            [
                jnp.where(key_row > query_row, scores[:, 0:BLK], -1e30),
                scores[:, BLK:WINDOW],
                jnp.where(key_row <= query_row, scores[:, WINDOW:KEYS], -1e30),
            ],
            axis=1,
        )
        weights = jnp.exp2(scores - jnp.max(scores, axis=1, keepdims=True))
        total = jnp.sum(weights, axis=1, keepdims=True)
        mixed = jnp.dot(
            weights.astype(BF), kv[1, start : start + KEYS, :], preferred_element_type=F32
        )
        ho[b, 0] = (mixed / total).astype(BF)

        @pl.when(core == 1)
        def _():
            send_right(b, 0).start()
            send_left(b, 0).start()

        @pl.when(core == 0)
        def _():
            enter_right(b).start()
            enter_left(b).start()


    @pl.when(jnp.logical_not(late))
    def _():
        spread()

    def step(hop):
        for b in order:
            send_right(b, hop - 1).wait_recv()
            if goes_right(b, hop):
                send_right(b, hop).start()
            send_left(b, hop - 1).wait_recv()
            if goes_left(b, hop):
                send_left(b, hop).start()

    def step2(hop):
        for b in order:
            send_right2(b, hop - 1).wait_recv()
            if goes_right(b, hop):
                send_right2(b, hop).start()
            hand(b, hop).start()
            send_left2(b, hop - 1).wait_recv()
            if goes_left(b, hop):
                send_left2(b, hop).start()
            hand(b, HALF + hop).start()

    def spread_on():
        for dist in range(1, NX):
            arrival_p2(dist).wait_recv()
            copy_sib(dist, mine).start()

    @pl.when(core == 1)
    def _():
        step(1)
        for hop in range(1, HALF):
            if hop + 1 < HALF:
                step(hop + 1)
            step2(hop)
            if hop == HALF - 2:
                spread_on()
        for b in order:
            send_right2(b, HALF - 1).wait_recv()
            hand(b, HALF).start()

    @pl.when(core == 0)
    def _():
        spread_on()
        for b in order:
            for i in range(1, NZ):
                if i != HALF:
                    hand(b, i).wait_recv()

    for dist in range(NX):
        copy_sib(dist, other).wait_recv()

    def copy_y(b):
        return copy(psend.at[b], precv.at[b], y_s.at[b], y_r.at[b], s, partner)

    theirs_at = pl.multiple_of((1 - yl) * MINE, 16)
    mine_at = pl.multiple_of(yl * MINE, 16)

    def product(b, slots, at):
        rows = jnp.concatenate([wbuf[i, pl.ds(at, MINE), :] for i in slots], axis=1)
        heads = jnp.concatenate([ho[b, i] for i in slots], axis=1)
        return lax.dot_general(rows, heads, NT, preferred_element_type=F32)

    early = [i for i in range(NZ) if i != HALF]
    for b in order:
        theirs = product(b, early, theirs_at)
        mine_part = product(b, early, mine_at)
        hand(b, HALF).wait_recv()
        psend[b] = (theirs + product(b, [HALF], theirs_at)).astype(BF)
        copy_y(b).start()
        own[b] = mine_part + product(b, [HALF], mine_at)
    for b in order:
        copy_y(b).wait_recv()
        out_ref[:, b * BLK : (b + 1) * BLK] = (own[b] + precv[b].astype(F32)).astype(BF)

    @pl.when(straight)
    def _():
        for j in order:
            copy_a(j).wait_send()

    @pl.when(around)
    def _():
        for j in order:
            copy_in(j).wait_send()

    @pl.when(passes)
    def _():
        for j in order:
            copy_on(j).wait_send()

    @pl.when(core == 0)
    def _():
        copy_c1().wait_send()

    @pl.when(has_prev)
    def _():
        for j in order:
            copy_b(j, yl).wait_send()

    @pl.when(has_prev & (core == 1))
    def _():
        for j in order:
            copy_c2(j, yl).wait_send()
            copy_c2(j, 1 - yl).wait_send()

    for j in range(HALF):
        copy_p1(j).wait_send()
    for dist in range(1, NX):
        copy_p2(dist).wait_send()
    for dist in range(NX):
        copy_sib(dist, mine).wait_send()
    @pl.when(core == 1)
    def _():
        for b in order:
            for hop in range(HALF):
                if goes_right(b, hop):
                    send_right(b, hop).wait_send()
                    if hop > 0:
                        send_right2(b, hop).wait_send()
                if goes_left(b, hop):
                    send_left(b, hop).wait_send()
                    if hop > 0:
                        send_left2(b, hop).wait_send()
            for i in range(1, NZ):
                hand(b, i).wait_send()

    @pl.when(core == 0)
    def _():
        for b in order:
            enter_right(b).wait_send()
            enter_left(b).wait_send()

    for b in order:
        copy_y(b).wait_send()


def per_device(hidden_in, norm_gain, query_weight, kv_weight, out_weight):
    index = np.arange(HD) % (HD // 2)
    freq = np.exp(-math.log(10000.0) * index * (2.0 / HD)).astype(np.float32)[None, :]
    any_space = pl.BlockSpec(memory_space=pl.ANY)
    vmem = pl.BlockSpec(memory_space=pltpu.VMEM)
    dma = pltpu.SemaphoreType.DMA
    return pl.pallas_call(
        kernel,
        out_shape=jax.ShapeDtypeStruct((MINE, ROWS), BF),
        in_specs=[any_space, vmem, any_space, any_space, any_space, vmem],
        out_specs=vmem,
        scratch_shapes=[
            pltpu.VMEM((NK, ROWS, KC), BF),
            pltpu.VMEM((NK, ROWS, KC), BF),
            pltpu.VMEM((D, HD), BF),
            pltpu.VMEM((NK, KC, 2 * HD), BF),
            pltpu.VMEM((HD, D), BF),
            pltpu.VMEM((D, HD), BF),
            pltpu.VMEM((NZ + 1, FEATS, HD), BF),
            pltpu.VMEM((2, 3 * ROWS, HD), BF),
            pltpu.VMEM((ROWS, HD), BF),
            pltpu.VMEM((NB, NZ, BLK, HD), BF),
            pltpu.VMEM((ROWS, 2 * HD), F32),
            pltpu.VMEM((ROWS, HD), F32),
            pltpu.VMEM((ROWS, HD), F32),
            pltpu.VMEM((ROWS, HD), F32),
            pltpu.VMEM((NB, MINE, BLK), BF),
            pltpu.VMEM((NB, MINE, BLK), BF),
            pltpu.VMEM((NB, MINE, BLK), F32),
            pltpu.VMEM((NB, BLK, HD), BF),
            pltpu.VMEM((NB, NZ, BLK, HD), BF),
            dma((NK,)), dma((NK,)), dma, dma,
            dma((NB,)), dma((NB,)), dma((NB,)), dma((NB,)),
            dma((1,)), dma((1,)), dma((2, NB)), dma((2, NB)),
            dma((HALF,)), dma((HALF,)), dma((NX,)), dma((NX,)), dma((NX,)), dma((NX,)),
            dma((NB, HALF)), dma((NB, HALF)), dma((NB, NZ)), dma((NB,)), dma((NB,)),
            dma((2, NB)), dma((NB,)),
            dma((NB, HALF)), dma((NB, HALF)), dma((NB, NZ)), dma((NB, NZ)),
        ],
        compiler_params=pltpu.CompilerParams(
            collective_id=0, has_side_effects=True, vmem_limit_bytes=60 * 1024 * 1024
        ),
    )(
        hidden_in, norm_gain, query_weight, kv_weight, out_weight, jnp.asarray(freq),
    )


def solution(mesh):
    in_specs = (P("seq", None), P(), P(None, "mp"), P(None, "mp"), P("mp", None))
    out_specs = P("mp", "seq")
    return jax.shard_map(
        per_device, mesh=mesh, in_specs=in_specs, out_specs=out_specs, check_vma=False
    )
```

```python
import math

import jax
import jax.numpy as jnp
import numpy as np
from jax import lax
from jax.experimental import pallas as pl
from jax.experimental.pallas import tpu as pltpu
from jax.sharding import PartitionSpec as P

MESH = pl.DeviceIdType.MESH
BF = jnp.bfloat16
F32 = jnp.float32

D = 5376
HD = 128
WINDOW = 1024
ROWS = 512
NZ = 12
NX = 4
HALF = NZ // 2
FEATS = D // NZ
MINE = FEATS // 2
QUARTER = FEATS // NX
NK = 7
KC = D // NK
AHEAD = 4
NB = 4
BLK = ROWS // NB
KEYS = WINDOW + BLK
SCALE = math.log2(math.e) / math.sqrt(168.0)

NT = (((1,), (1,)), ((), ()))


def kernel(
    x_hbm, gain_ref, wq_hbm, wkv_hbm, wo_hbm, freq_ref, out_ref,
    xb, xg, wqb, wkvb, wob, wt, wbuf, kv, qb, ho, acc, ss, rc, rs, psend, precv, own, rel, h2,
    ld_x, ld_kv, ld_q, ld_o,
    a_s, a_r, b_s, b_r, c1_s, c1_r, c2_s, c2_r,
    p1_s, p1_r, p2_s, p2_r, p3_s, p3_r,
    r_s, l_s, g_r, y_s, y_r, f_s, f_r,
    r2_s, l2_s, g2_r, d_s,
):
    s = lax.axis_index("seq")
    m = lax.axis_index("mp")
    nseq = lax.axis_size("seq")
    z = m // 2
    yl = m % 2
    core = s % 2
    x = (s // 2) % NX
    partner = m + 1 - 2 * yl
    sibling = s + 1 - 2 * core
    has_prev = s >= 2
    has_next = s < nseq - 2
    turns = x == NX - 1
    passes = (x == 0) & (s < nseq - 2 * NX) & (yl == 1)
    passed = (x == 0) & has_prev & (yl == 0)

    def at_z(dist):
        return ((z + dist + NZ) % NZ) * 2 + yl

    def at_x(dist):
        return s + 2 * ((x + dist) % NX - x)

    def copy(src, dst, ssem, rsem, seq, mp):
        return pltpu.make_async_remote_copy(
            src_ref=src, dst_ref=dst, send_sem=ssem, recv_sem=rsem,
            device_id=(seq, mp), device_id_type=MESH,
        )

    load_o = pltpu.make_async_copy(wo_hbm, wob, ld_o)
    load_q = pltpu.make_async_copy(wq_hbm, wqb, ld_q)

    def load_x(k):
        return pltpu.make_async_copy(x_hbm.at[:, pl.ds(k * KC, KC)], xb.at[k], ld_x.at[k])

    def load_kv(k):
        return pltpu.make_async_copy(wkv_hbm.at[pl.ds(k * KC, KC), :], wkvb.at[k], ld_kv.at[k])

    def load(k):
        if k < NK:
            load_x(k).start()
            load_kv(k).start()
        elif k == NK:
            load_o.start()
        elif k == NK + 1:
            load_q.start()

    for k in range(AHEAD):
        load(k)

    barrier = pltpu.get_barrier_semaphore()

    def greet(seq, mp):
        pl.semaphore_signal(barrier, inc=1, device_id=(seq, mp), device_id_type=MESH)

    for dist in range(1, NZ):
        greet(s, at_z(dist))
    for dist in range(1, NX):
        greet(at_x(dist), m)
    greet(sibling, m)
    greet(sibling, at_z(1))
    greet(sibling, at_z(-1))
    greet(s, partner)

    @pl.when(has_prev)
    def _():
        greet(s - 2, m)

    @pl.when(has_next)
    def _():
        greet(s + 2, m)

    @pl.when(passes)
    def _():
        greet(s + 2 * NX, m - 1)

    @pl.when(passed)
    def _():
        greet(s - 2 * NX, m + 1)

    lane = lax.broadcasted_iota(jnp.int32, (32, HD), 1)
    sign = jnp.where(lane < HD // 2, -1.0, 1.0).astype(F32)
    row = lax.broadcasted_iota(jnp.int32, (48, HD), 0)
    place = jnp.where(row < 16, ROWS * s + 32 * row, row - 16).astype(F32)
    angle = place * freq_ref[...]
    cosine = jnp.cos(angle)
    sine = jnp.sin(angle)
    cos_low = cosine[16:48, :]
    sin_low = sine[16:48, :]
    for a in range(16):
        cos_high = cosine[a : a + 1, :]
        sin_high = sine[a : a + 1, :]
        rc[32 * a : 32 * a + 32, :] = cos_high * cos_low - sin_high * sin_low
        rs[32 * a : 32 * a + 32, :] = (sin_high * cos_low + cos_high * sin_low) * sign

    @pl.when(s == 0)
    def _():
        kv[:, 0 : 2 * ROWS, :] = jnp.zeros((2, 2 * ROWS, HD), BF)

    @pl.when(s == 1)
    def _():
        kv[:, 0:ROWS, :] = jnp.zeros((2, ROWS, HD), BF)

    def scale(k):
        gain = gain_ref[pl.ds(k * KC, KC)].reshape(1, KC)
        for r in range(0, ROWS, 16):
            wide = xb[k, r : r + 16, :].astype(F32)
            square = wide * wide
            part = square[:, 0:HD]
            for c in range(HD, KC, HD):
                part = part + square[:, c : c + HD]
            if k == 0:
                ss[r : r + 16, :] = part
            else:
                ss[r : r + 16, :] += part
            xg[k, r : r + 16, :] = (wide * gain).astype(BF)

    def arrive(k):
        load_x(k).wait()
        load_kv(k).wait()
        load(k + AHEAD)

    arrive(0)
    scale(0)
    for k in range(NK):
        if k + 1 < NK:
            arrive(k + 1)
            scale(k + 1)
        part = jnp.dot(xg[k], wkvb[k], preferred_element_type=F32)
        if k == 0:
            acc[...] = part
        else:
            acc[...] += part
    inverse = lax.rsqrt(jnp.sum(ss[...], axis=1, keepdims=True) * (1.0 / D) + 1e-06)

    def rope(t):
        return t * rc[...] + pltpu.roll(t, HD // 2, 1) * rs[...]

    kv[0, 2 * ROWS : 3 * ROWS, :] = rope(acc[:, 0:HD] * inverse).astype(BF)
    kv[1, 2 * ROWS : 3 * ROWS, :] = (acc[:, HD : 2 * HD] * inverse).astype(BF)

    pl.semaphore_wait(
        barrier,
        (NZ - 1) + (NX - 1) + 4 + has_prev.astype(jnp.int32) + has_next.astype(jnp.int32)
        + passes.astype(jnp.int32) + passed.astype(jnp.int32),
    )

    def copy_a(j):
        return copy(
            kv.at[yl, pl.ds(2 * ROWS + j * BLK, BLK), :], kv.at[yl, pl.ds(j * BLK, BLK), :],
            a_s.at[j], a_r.at[j], s + 2, m,
        )

    def copy_b(j, half):
        block = kv.at[half, pl.ds(j * BLK, BLK), :]
        return copy(block, block, b_s.at[j], b_r.at[j], s, partner)

    def copy_c1():
        return copy(
            kv.at[:, pl.ds(2 * ROWS, ROWS), :], kv.at[:, pl.ds(ROWS, ROWS), :],
            c1_s.at[0], c1_r.at[0], sibling, m,
        )

    def copy_c2(j, half):
        return copy(
            kv.at[half, pl.ds(j * BLK, BLK), :], kv.at[half, pl.ds(ROWS + j * BLK, BLK), :],
            c2_s.at[half, j], c2_r.at[half, j], sibling, m,
        )

    order = tuple(range(NB - 1, -1, -1))

    def copy_in(j):
        return copy(
            kv.at[0, pl.ds(2 * ROWS + j * BLK, BLK), :], rel.at[j], f_s.at[0, j], f_r.at[j], at_x(1), m,
        )

    def copy_on(j):
        return copy(
            rel.at[j], kv.at[0, pl.ds(j * BLK, BLK), :], f_s.at[1, j], a_r.at[j], s + 2 * NX, m - 1,
        )

    straight = has_next & (jnp.logical_not(turns) | (yl == 1))
    around = has_next & turns & (yl == 1)

    def send_on(which):
        @pl.when(straight)
        def _():
            for j in which:
                copy_a(j).start()

        @pl.when(around)
        def _():
            for j in which:
                copy_in(j).start()

    @pl.when(core == 1)
    def _():
        send_on(order)

    @pl.when(core == 0)
    def _():
        send_on(order[:1])
        copy_c1().start()

    load_o.wait()
    for f in range(D // HD):
        wt[f * HD : (f + 1) * HD, :] = wob[:, f * HD : (f + 1) * HD].T

    def copy_p1(j):
        dist = (j + 1) * (1 - 2 * core)
        plane = (z + dist + NZ) % NZ
        slot = 1 + j + HALF * core
        return copy(
            wt.at[pl.ds(pl.multiple_of(plane * FEATS + x * QUARTER, 16), QUARTER), :],
            wbuf.at[slot, pl.ds(pl.multiple_of(x * QUARTER, 16), QUARTER), :],
            p1_s.at[j], p1_r.at[j], s, plane * 2 + yl,
        )

    for j in range(HALF):
        copy_p1(j).start()
    wbuf[0] = wt[pl.ds(pl.multiple_of(z * FEATS, 16), FEATS), :]

    load_q.wait()
    queries = jnp.dot(xg[0], wqb[0:KC, :], preferred_element_type=F32)
    for k in range(1, NK):
        queries = queries + jnp.dot(
            xg[k], wqb[k * KC : (k + 1) * KC, :], preferred_element_type=F32
        )
    qb[...] = (rope(queries * inverse) * SCALE).astype(BF)

    @pl.when(core == 0)
    def _():
        send_on(order[1:])

    def quarter(slot, dist):
        rows = pl.ds(pl.multiple_of(((x - dist + NX) % NX) * QUARTER, 16), QUARTER)
        return wbuf.at[pl.ds(slot, HALF), rows, :]

    mine = 1 + HALF * core
    other = 1 + HALF * (1 - core)

    def copy_p2(dist):
        return copy(quarter(mine, 0), quarter(mine, 0), p2_s.at[dist], p2_r.at[dist], at_x(dist), m)

    def arrival_p2(dist):
        return copy(quarter(mine, dist), quarter(mine, dist), p2_s.at[dist], p2_r.at[dist], at_x(-dist), m)

    def copy_sib(dist, slot):
        return copy(quarter(slot, dist), quarter(slot, dist), p3_s.at[dist], p3_r.at[dist], sibling, m)

    def spread():
        for j in range(HALF):
            copy_p1(j).wait_recv()
        for dist in range(1, NX):
            copy_p2(dist).start()
        copy_sib(0, mine).start()

    @pl.when(passes)
    def _():
        for j in order:
            copy_in(j).wait_recv()
            copy_on(j).start()

    @pl.when(has_prev & (core == 1))
    def _():
        for j in order:
            copy_a(j).wait_recv()
            copy_b(j, yl).start()
            copy_c2(j, yl).start()
        for j in order:
            copy_b(j, 1 - yl).wait_recv()
            copy_c2(j, 1 - yl).start()

    @pl.when(has_prev & (core == 0))
    def _():
        for j in order:
            copy_a(j).wait_recv()
            copy_b(j, yl).start()
        for j in order:
            copy_c2(j, yl).wait_recv()
            copy_c2(j, 1 - yl).wait_recv()

    @pl.when(core == 1)
    def _():
        copy_c1().wait_recv()

    right, left = at_z(1), at_z(-1)

    def send_right(b, d):
        return copy(ho.at[b, d], ho.at[b, d + 1], r_s.at[b, d], g_r.at[b, d + 1], s, right)

    def send_left(b, e):
        to = HALF if e == HALF - 1 else HALF + e + 1
        frm = 0 if e == 0 else HALF + e
        return copy(ho.at[b, frm], ho.at[b, to], l_s.at[b, e], g_r.at[b, to], s, left)

    by_second = order[NB // 2 :]

    def send_right2(b, d):
        return copy(h2.at[b, d], h2.at[b, d + 1], r2_s.at[b, d], g2_r.at[b, d + 1], s, right)

    def send_left2(b, e):
        to = HALF if e == HALF - 1 else HALF + e + 1
        return copy(h2.at[b, HALF + e], h2.at[b, to], l2_s.at[b, e], g2_r.at[b, to], s, left)

    def enter_right(b):
        return copy(ho.at[b, 0], h2.at[b, 1], r2_s.at[b, 0], g2_r.at[b, 1], sibling, right)

    def enter_left(b):
        return copy(ho.at[b, 0], h2.at[b, HALF + 1], l2_s.at[b, 0], g2_r.at[b, HALF + 1], sibling, left)

    def hand(b, i):
        return copy(h2.at[b, i], ho.at[b, i], d_s.at[b, i], g_r.at[b, i], sibling, m)

    def goes_right(b, hop):
        return hop + 1 < HALF or b < NB // 2

    def goes_left(b, hop):
        return hop + 1 < HALF or b >= NB // 2

    first_key = jnp.maximum(WINDOW - ROWS * s, 0)
    query_row = lax.broadcasted_iota(jnp.int32, (BLK, BLK), 0)
    key_row = lax.broadcasted_iota(jnp.int32, (BLK, BLK), 1)
    column = lax.broadcasted_iota(jnp.int32, (1, KEYS), 1)
    for b in order:
        start = b * BLK

        @pl.when(has_prev & (core == 0))
        def _():
            copy_b(b, 1 - yl).wait_recv()

        scores = lax.dot_general(
            qb[start : start + BLK, :], kv[0, start : start + KEYS, :], NT,
            preferred_element_type=F32,
        )
        exists = column + start >= first_key
        scores = jnp.where(exists, scores, -1e30)
        scores = jnp.concatenate(
            [
                jnp.where(key_row > query_row, scores[:, 0:BLK], -1e30),
                scores[:, BLK:WINDOW],
                jnp.where(key_row <= query_row, scores[:, WINDOW:KEYS], -1e30),
            ],
            axis=1,
        )
        weights = jnp.exp2(scores - jnp.max(scores, axis=1, keepdims=True))
        total = jnp.sum(weights, axis=1, keepdims=True)
        mixed = jnp.dot(
            weights.astype(BF), kv[1, start : start + KEYS, :], preferred_element_type=F32
        )
        ho[b, 0] = (mixed / total).astype(BF)

        def first_hop():
            send_right(b, 0).start()
            send_left(b, 0).start()

        if b in by_second:
            pl.when(core == 1)(first_hop)

            @pl.when(core == 0)
            def _():
                enter_right(b).start()
                enter_left(b).start()
        else:
            first_hop()


    spread()

    def step(hop, blocks):
        for b in blocks:
            send_right(b, hop - 1).wait_recv()
            if goes_right(b, hop):
                send_right(b, hop).start()
            send_left(b, hop - 1).wait_recv()
            if goes_left(b, hop):
                send_left(b, hop).start()

    def step2(hop):
        for b in by_second:
            send_right2(b, hop - 1).wait_recv()
            if goes_right(b, hop):
                send_right2(b, hop).start()
            hand(b, hop).start()
            send_left2(b, hop - 1).wait_recv()
            if goes_left(b, hop):
                send_left2(b, hop).start()
            hand(b, HALF + hop).start()

    def spread_on():
        for dist in range(1, NX):
            arrival_p2(dist).wait_recv()
            copy_sib(dist, mine).start()

    @pl.when(core == 1)
    def _():
        step(1, order)
        for hop in range(1, HALF):
            if hop + 1 < HALF:
                step(hop + 1, order)
            step2(hop)
            if hop == 3:
                spread_on()
        for b in by_second:
            send_right2(b, HALF - 1).wait_recv()
            hand(b, HALF).start()

    @pl.when(core == 0)
    def _():
        for hop in range(1, HALF):
            step(hop, order[: NB // 2])
            if hop == 3:
                spread_on()
        for b in by_second:
            for i in range(1, NZ):
                if i != HALF:
                    hand(b, i).wait_recv()

    for dist in range(NX):
        copy_sib(dist, other).wait_recv()

    def copy_y(b):
        return copy(psend.at[b], precv.at[b], y_s.at[b], y_r.at[b], s, partner)

    theirs_at = pl.multiple_of((1 - yl) * MINE, 16)
    mine_at = pl.multiple_of(yl * MINE, 16)

    def product(b, slots, at):
        rows = jnp.concatenate([wbuf[i, pl.ds(at, MINE), :] for i in slots], axis=1)
        heads = jnp.concatenate([ho[b, i] for i in slots], axis=1)
        return lax.dot_general(rows, heads, NT, preferred_element_type=F32)

    early = [i for i in range(NZ) if i != HALF]
    for b in order:
        theirs = product(b, early, theirs_at)
        mine_part = product(b, early, mine_at)
        hand(b, HALF).wait_recv()
        psend[b] = (theirs + product(b, [HALF], theirs_at)).astype(BF)
        copy_y(b).start()
        own[b] = mine_part + product(b, [HALF], mine_at)
    for b in order:
        copy_y(b).wait_recv()
        out_ref[:, b * BLK : (b + 1) * BLK] = (own[b] + precv[b].astype(F32)).astype(BF)

    @pl.when(straight)
    def _():
        for j in order:
            copy_a(j).wait_send()

    @pl.when(around)
    def _():
        for j in order:
            copy_in(j).wait_send()

    @pl.when(passes)
    def _():
        for j in order:
            copy_on(j).wait_send()

    @pl.when(core == 0)
    def _():
        copy_c1().wait_send()

    @pl.when(has_prev)
    def _():
        for j in order:
            copy_b(j, yl).wait_send()

    @pl.when(has_prev & (core == 1))
    def _():
        for j in order:
            copy_c2(j, yl).wait_send()
            copy_c2(j, 1 - yl).wait_send()

    for j in range(HALF):
        copy_p1(j).wait_send()
    for dist in range(1, NX):
        copy_p2(dist).wait_send()
    for dist in range(NX):
        copy_sib(dist, mine).wait_send()
    def ring_left(blocks):
        for b in blocks:
            for hop in range(HALF):
                if goes_right(b, hop):
                    send_right(b, hop).wait_send()
                if goes_left(b, hop):
                    send_left(b, hop).wait_send()

    ring_left(order[: NB // 2])

    @pl.when(core == 1)
    def _():
        ring_left(by_second)
        for b in by_second:
            for hop in range(1, HALF):
                if goes_right(b, hop):
                    send_right2(b, hop).wait_send()
                if goes_left(b, hop):
                    send_left2(b, hop).wait_send()
            for i in range(1, NZ):
                hand(b, i).wait_send()

    @pl.when(core == 0)
    def _():
        for b in by_second:
            enter_right(b).wait_send()
            enter_left(b).wait_send()

    for b in order:
        copy_y(b).wait_send()


def per_device(hidden_in, norm_gain, query_weight, kv_weight, out_weight):
    index = np.arange(HD) % (HD // 2)
    freq = np.exp(-math.log(10000.0) * index * (2.0 / HD)).astype(np.float32)[None, :]
    any_space = pl.BlockSpec(memory_space=pl.ANY)
    vmem = pl.BlockSpec(memory_space=pltpu.VMEM)
    dma = pltpu.SemaphoreType.DMA
    return pl.pallas_call(
        kernel,
        out_shape=jax.ShapeDtypeStruct((MINE, ROWS), BF),
        in_specs=[any_space, vmem, any_space, any_space, any_space, vmem],
        out_specs=vmem,
        scratch_shapes=[
            pltpu.VMEM((NK, ROWS, KC), BF),
            pltpu.VMEM((NK, ROWS, KC), BF),
            pltpu.VMEM((D, HD), BF),
            pltpu.VMEM((NK, KC, 2 * HD), BF),
            pltpu.VMEM((HD, D), BF),
            pltpu.VMEM((D, HD), BF),
            pltpu.VMEM((NZ + 1, FEATS, HD), BF),
            pltpu.VMEM((2, 3 * ROWS, HD), BF),
            pltpu.VMEM((ROWS, HD), BF),
            pltpu.VMEM((NB, NZ, BLK, HD), BF),
            pltpu.VMEM((ROWS, 2 * HD), F32),
            pltpu.VMEM((ROWS, HD), F32),
            pltpu.VMEM((ROWS, HD), F32),
            pltpu.VMEM((ROWS, HD), F32),
            pltpu.VMEM((NB, MINE, BLK), BF),
            pltpu.VMEM((NB, MINE, BLK), BF),
            pltpu.VMEM((NB, MINE, BLK), F32),
            pltpu.VMEM((NB, BLK, HD), BF),
            pltpu.VMEM((NB, NZ, BLK, HD), BF),
            dma((NK,)), dma((NK,)), dma, dma,
            dma((NB,)), dma((NB,)), dma((NB,)), dma((NB,)),
            dma((1,)), dma((1,)), dma((2, NB)), dma((2, NB)),
            dma((HALF,)), dma((HALF,)), dma((NX,)), dma((NX,)), dma((NX,)), dma((NX,)),
            dma((NB, HALF)), dma((NB, HALF)), dma((NB, NZ)), dma((NB,)), dma((NB,)),
            dma((2, NB)), dma((NB,)),
            dma((NB, HALF)), dma((NB, HALF)), dma((NB, NZ)), dma((NB, NZ)),
        ],
        compiler_params=pltpu.CompilerParams(
            collective_id=0, has_side_effects=True, vmem_limit_bytes=60 * 1024 * 1024
        ),
    )(
        hidden_in, norm_gain, query_weight, kv_weight, out_weight, jnp.asarray(freq),
    )


def solution(mesh):
    in_specs = (P("seq", None), P(), P(None, "mp"), P(None, "mp"), P("mp", None))
    out_specs = P("mp", "seq")
    return jax.shard_map(
        per_device, mesh=mesh, in_specs=in_specs, out_specs=out_specs, check_vma=False
    )
```

```python
import math

import jax
import jax.numpy as jnp
import numpy as np
from jax import lax
from jax.experimental import pallas as pl
from jax.experimental.pallas import tpu as pltpu
from jax.sharding import PartitionSpec as P

MESH = pl.DeviceIdType.MESH
BF = jnp.bfloat16
F32 = jnp.float32

D = 5376
HD = 128
WINDOW = 1024
ROWS = 512
NZ = 12
NX = 4
HALF = NZ // 2
FEATS = D // NZ
MINE = FEATS // 2
QUARTER = FEATS // NX
NK = 7
KC = D // NK
AHEAD = 4
NB = 4
BLK = ROWS // NB
KEYS = WINDOW + BLK
SCALE = math.log2(math.e) / math.sqrt(168.0)

NT = (((1,), (1,)), ((), ()))


def kernel(
    x_hbm, gain_ref, wq_hbm, wkv_hbm, wo_hbm, freq_ref, out_ref,
    xb, xg, wqb, wkvb, wob, wt, wbuf, kv, qb, ho, acc, ss, rc, rs, psend, precv, own, rel,
    ld_x, ld_kv, ld_q, ld_o,
    a_s, a_r, b_s, b_r, c1_s, c1_r, c2_s, c2_r,
    p1_s, p1_r, p2_s, p2_r, p3_s, p3_r,
    r_s, l_s, g_r, y_s, y_r, f_s, f_r,
):
    s = lax.axis_index("seq")
    m = lax.axis_index("mp")
    nseq = lax.axis_size("seq")
    z = m // 2
    yl = m % 2
    core = s % 2
    x = (s // 2) % NX
    partner = m + 1 - 2 * yl
    sibling = s + 1 - 2 * core
    has_prev = s >= 2
    has_next = s < nseq - 2
    turns = x == NX - 1
    passes = (x == 0) & (s < nseq - 2 * NX) & (yl == 1)
    passed = (x == 0) & has_prev & (yl == 0)

    def at_z(dist):
        return ((z + dist + NZ) % NZ) * 2 + yl

    def at_x(dist):
        return s + 2 * ((x + dist) % NX - x)

    def copy(src, dst, ssem, rsem, seq, mp):
        return pltpu.make_async_remote_copy(
            src_ref=src, dst_ref=dst, send_sem=ssem, recv_sem=rsem,
            device_id=(seq, mp), device_id_type=MESH,
        )

    load_o = pltpu.make_async_copy(wo_hbm, wob, ld_o)
    load_q = pltpu.make_async_copy(wq_hbm, wqb, ld_q)

    def load_x(k):
        return pltpu.make_async_copy(x_hbm.at[:, pl.ds(k * KC, KC)], xb.at[k], ld_x.at[k])

    def load_kv(k):
        return pltpu.make_async_copy(wkv_hbm.at[pl.ds(k * KC, KC), :], wkvb.at[k], ld_kv.at[k])

    def load(k):
        if k < NK:
            load_x(k).start()
            load_kv(k).start()
        elif k == NK:
            load_o.start()
        elif k == NK + 1:
            load_q.start()

    for k in range(AHEAD):
        load(k)

    barrier = pltpu.get_barrier_semaphore()

    def greet(seq, mp):
        pl.semaphore_signal(barrier, inc=1, device_id=(seq, mp), device_id_type=MESH)

    for dist in range(1, NZ):
        greet(s, at_z(dist))
    for dist in range(1, NX):
        greet(at_x(dist), m)
    greet(sibling, m)
    greet(s, partner)

    @pl.when(has_prev)
    def _():
        greet(s - 2, m)

    @pl.when(has_next)
    def _():
        greet(s + 2, m)

    @pl.when(passes)
    def _():
        greet(s + 2 * NX, m - 1)

    @pl.when(passed)
    def _():
        greet(s - 2 * NX, m + 1)

    lane = lax.broadcasted_iota(jnp.int32, (32, HD), 1)
    sign = jnp.where(lane < HD // 2, -1.0, 1.0).astype(F32)
    row = lax.broadcasted_iota(jnp.int32, (48, HD), 0)
    place = jnp.where(row < 16, ROWS * s + 32 * row, row - 16).astype(F32)
    angle = place * freq_ref[...]
    cosine = jnp.cos(angle)
    sine = jnp.sin(angle)
    cos_low = cosine[16:48, :]
    sin_low = sine[16:48, :]
    for a in range(16):
        cos_high = cosine[a : a + 1, :]
        sin_high = sine[a : a + 1, :]
        rc[32 * a : 32 * a + 32, :] = cos_high * cos_low - sin_high * sin_low
        rs[32 * a : 32 * a + 32, :] = (sin_high * cos_low + cos_high * sin_low) * sign

    @pl.when(s == 0)
    def _():
        kv[:, 0 : 2 * ROWS, :] = jnp.zeros((2, 2 * ROWS, HD), BF)

    @pl.when(s == 1)
    def _():
        kv[:, 0:ROWS, :] = jnp.zeros((2, ROWS, HD), BF)

    def scale(k):
        gain = gain_ref[pl.ds(k * KC, KC)].reshape(1, KC)
        for r in range(0, ROWS, 16):
            wide = xb[k, r : r + 16, :].astype(F32)
            square = wide * wide
            part = square[:, 0:HD]
            for c in range(HD, KC, HD):
                part = part + square[:, c : c + HD]
            if k == 0:
                ss[r : r + 16, :] = part
            else:
                ss[r : r + 16, :] += part
            xg[k, r : r + 16, :] = (wide * gain).astype(BF)

    def arrive(k):
        load_x(k).wait()
        load_kv(k).wait()
        load(k + AHEAD)

    arrive(0)
    scale(0)
    for k in range(NK):
        if k + 1 < NK:
            arrive(k + 1)
            scale(k + 1)
        part = jnp.dot(xg[k], wkvb[k], preferred_element_type=F32)
        if k == 0:
            acc[...] = part
        else:
            acc[...] += part
    inverse = lax.rsqrt(jnp.sum(ss[...], axis=1, keepdims=True) * (1.0 / D) + 1e-06)

    def rope(t):
        return t * rc[...] + pltpu.roll(t, HD // 2, 1) * rs[...]

    kv[0, 2 * ROWS : 3 * ROWS, :] = rope(acc[:, 0:HD] * inverse).astype(BF)
    kv[1, 2 * ROWS : 3 * ROWS, :] = (acc[:, HD : 2 * HD] * inverse).astype(BF)

    pl.semaphore_wait(
        barrier,
        (NZ - 1) + (NX - 1) + 2 + has_prev.astype(jnp.int32) + has_next.astype(jnp.int32)
        + passes.astype(jnp.int32) + passed.astype(jnp.int32),
    )

    def copy_a(j):
        return copy(
            kv.at[yl, pl.ds(2 * ROWS + j * BLK, BLK), :], kv.at[yl, pl.ds(j * BLK, BLK), :],
            a_s.at[j], a_r.at[j], s + 2, m,
        )

    def copy_b(j, half):
        block = kv.at[half, pl.ds(j * BLK, BLK), :]
        return copy(block, block, b_s.at[j], b_r.at[j], s, partner)

    def copy_c1():
        return copy(
            kv.at[:, pl.ds(2 * ROWS, ROWS), :], kv.at[:, pl.ds(ROWS, ROWS), :],
            c1_s.at[0], c1_r.at[0], sibling, m,
        )

    def copy_c2(j, half):
        return copy(
            kv.at[half, pl.ds(j * BLK, BLK), :], kv.at[half, pl.ds(ROWS + j * BLK, BLK), :],
            c2_s.at[half, j], c2_r.at[half, j], sibling, m,
        )

    order = tuple(range(NB - 1, -1, -1))

    def copy_in(j):
        return copy(
            kv.at[0, pl.ds(2 * ROWS + j * BLK, BLK), :], rel.at[j], f_s.at[0, j], f_r.at[j], at_x(1), m,
        )

    def copy_on(j):
        return copy(
            rel.at[j], kv.at[0, pl.ds(j * BLK, BLK), :], f_s.at[1, j], a_r.at[j], s + 2 * NX, m - 1,
        )

    straight = has_next & (jnp.logical_not(turns) | (yl == 1))
    around = has_next & turns & (yl == 1)

    def send_on(which):
        @pl.when(straight)
        def _():
            for j in which:
                copy_a(j).start()

        @pl.when(around)
        def _():
            for j in which:
                copy_in(j).start()

    @pl.when(core == 1)
    def _():
        send_on(order)

    @pl.when(core == 0)
    def _():
        send_on(order[:1])
        copy_c1().start()

    load_o.wait()
    for f in range(D // HD):
        wt[f * HD : (f + 1) * HD, :] = wob[:, f * HD : (f + 1) * HD].T

    def copy_p1(j):
        dist = (j + 1) * (1 - 2 * core)
        plane = (z + dist + NZ) % NZ
        slot = 1 + j + HALF * core
        return copy(
            wt.at[pl.ds(pl.multiple_of(plane * FEATS + x * QUARTER, 16), QUARTER), :],
            wbuf.at[slot, pl.ds(pl.multiple_of(x * QUARTER, 16), QUARTER), :],
            p1_s.at[j], p1_r.at[j], s, plane * 2 + yl,
        )

    for j in range(HALF):
        copy_p1(j).start()
    wbuf[0] = wt[pl.ds(pl.multiple_of(z * FEATS, 16), FEATS), :]

    load_q.wait()
    queries = jnp.dot(xg[0], wqb[0:KC, :], preferred_element_type=F32)
    for k in range(1, NK):
        queries = queries + jnp.dot(
            xg[k], wqb[k * KC : (k + 1) * KC, :], preferred_element_type=F32
        )
    qb[...] = (rope(queries * inverse) * SCALE).astype(BF)

    @pl.when(core == 0)
    def _():
        send_on(order[1:])

    @pl.when(passes)
    def _():
        for j in order:
            copy_in(j).wait_recv()
            copy_on(j).start()

    @pl.when(has_prev & (core == 1))
    def _():
        for j in order:
            copy_a(j).wait_recv()
            copy_b(j, yl).start()
            copy_c2(j, yl).start()
        for j in order:
            copy_b(j, 1 - yl).wait_recv()
            copy_c2(j, 1 - yl).start()

    @pl.when(has_prev & (core == 0))
    def _():
        for j in order:
            copy_a(j).wait_recv()
            copy_b(j, yl).start()
        for j in order:
            copy_c2(j, yl).wait_recv()
            copy_c2(j, 1 - yl).wait_recv()

    @pl.when(core == 1)
    def _():
        copy_c1().wait_recv()

    right, left = at_z(1), at_z(-1)

    def send_right(b, d):
        return copy(ho.at[b, d], ho.at[b, d + 1], r_s.at[b, d], g_r.at[b, d + 1], s, right)

    def send_left(b, e):
        frm = 0 if e == 0 else HALF + e
        to = HALF + e + 1
        return copy(ho.at[b, frm], ho.at[b, to], l_s.at[b, e], g_r.at[b, to], s, left)

    def send_last(b):
        frm, to = (HALF - 2, at_z(2)) if b < NB // 2 else (NZ - 2, at_z(-2))
        sem = (r_s if b < NB // 2 else l_s).at[b, HALF - 1]
        return copy(ho.at[b, frm], ho.at[b, HALF], sem, g_r.at[b, HALF], s, to)

    first_key = jnp.maximum(WINDOW - ROWS * s, 0)
    query_row = lax.broadcasted_iota(jnp.int32, (BLK, BLK), 0)
    key_row = lax.broadcasted_iota(jnp.int32, (BLK, BLK), 1)
    column = lax.broadcasted_iota(jnp.int32, (1, KEYS), 1)
    for b in order:
        start = b * BLK

        @pl.when(has_prev & (core == 0))
        def _():
            copy_b(b, 1 - yl).wait_recv()

        scores = lax.dot_general(
            qb[start : start + BLK, :], kv[0, start : start + KEYS, :], NT,
            preferred_element_type=F32,
        )
        exists = column + start >= first_key
        scores = jnp.where(exists, scores, -1e30)
        scores = jnp.concatenate(
            [
                jnp.where(key_row > query_row, scores[:, 0:BLK], -1e30),
                scores[:, BLK:WINDOW],
                jnp.where(key_row <= query_row, scores[:, WINDOW:KEYS], -1e30),
            ],
            axis=1,
        )
        weights = jnp.exp2(scores - jnp.max(scores, axis=1, keepdims=True))
        total = jnp.sum(weights, axis=1, keepdims=True)
        mixed = jnp.dot(
            weights.astype(BF), kv[1, start : start + KEYS, :], preferred_element_type=F32
        )
        ho[b, 0] = (mixed / total).astype(BF)
        send_right(b, 0).start()
        send_left(b, 0).start()

    def quarter(slot, dist):
        rows = pl.ds(pl.multiple_of(((x - dist + NX) % NX) * QUARTER, 16), QUARTER)
        return wbuf.at[pl.ds(slot, HALF), rows, :]

    mine = 1 + HALF * core
    other = 1 + HALF * (1 - core)

    def copy_p2(dist):
        return copy(quarter(mine, 0), quarter(mine, 0), p2_s.at[dist], p2_r.at[dist], at_x(dist), m)

    def arrival_p2(dist):
        return copy(quarter(mine, dist), quarter(mine, dist), p2_s.at[dist], p2_r.at[dist], at_x(-dist), m)

    def copy_sib(dist, slot):
        return copy(quarter(slot, dist), quarter(slot, dist), p3_s.at[dist], p3_r.at[dist], sibling, m)

    for j in range(HALF):
        copy_p1(j).wait_recv()
    for dist in range(1, NX):
        copy_p2(dist).start()
    copy_sib(0, mine).start()

    for hop in range(1, HALF):
        for b in order:
            send_right(b, hop - 1).wait_recv()
            if hop + 2 == HALF and b < NB // 2:
                send_last(b).start()
            if hop + 1 < HALF:
                send_right(b, hop).start()
            send_left(b, hop - 1).wait_recv()
            if hop + 2 == HALF and b >= NB // 2:
                send_last(b).start()
            if hop + 1 < HALF:
                send_left(b, hop).start()
        if hop == 3:
            for dist in range(1, NX):
                arrival_p2(dist).wait_recv()
                copy_sib(dist, mine).start()
    for dist in range(NX):
        copy_sib(dist, other).wait_recv()

    def copy_y(b):
        return copy(psend.at[b], precv.at[b], y_s.at[b], y_r.at[b], s, partner)

    theirs_at = pl.multiple_of((1 - yl) * MINE, 16)
    mine_at = pl.multiple_of(yl * MINE, 16)

    def product(b, slots, at):
        rows = jnp.concatenate([wbuf[i, pl.ds(at, MINE), :] for i in slots], axis=1)
        heads = jnp.concatenate([ho[b, i] for i in slots], axis=1)
        return lax.dot_general(rows, heads, NT, preferred_element_type=F32)

    early = [i for i in range(NZ) if i != HALF]
    for b in order:
        theirs = product(b, early, theirs_at)
        mine_part = product(b, early, mine_at)
        send_last(b).wait_recv()
        psend[b] = (theirs + product(b, [HALF], theirs_at)).astype(BF)
        copy_y(b).start()
        own[b] = mine_part + product(b, [HALF], mine_at)
    for b in order:
        copy_y(b).wait_recv()
        out_ref[:, b * BLK : (b + 1) * BLK] = (own[b] + precv[b].astype(F32)).astype(BF)

    @pl.when(straight)
    def _():
        for j in order:
            copy_a(j).wait_send()

    @pl.when(around)
    def _():
        for j in order:
            copy_in(j).wait_send()

    @pl.when(passes)
    def _():
        for j in order:
            copy_on(j).wait_send()

    @pl.when(core == 0)
    def _():
        copy_c1().wait_send()

    @pl.when(has_prev)
    def _():
        for j in order:
            copy_b(j, yl).wait_send()

    @pl.when(has_prev & (core == 1))
    def _():
        for j in order:
            copy_c2(j, yl).wait_send()
            copy_c2(j, 1 - yl).wait_send()

    for j in range(HALF):
        copy_p1(j).wait_send()
    for dist in range(1, NX):
        copy_p2(dist).wait_send()
    for dist in range(NX):
        copy_sib(dist, mine).wait_send()
    for b in order:
        for hop in range(HALF - 1):
            send_right(b, hop).wait_send()
            send_left(b, hop).wait_send()
        send_last(b).wait_send()
        copy_y(b).wait_send()


def per_device(hidden_in, norm_gain, query_weight, kv_weight, out_weight):
    index = np.arange(HD) % (HD // 2)
    freq = np.exp(-math.log(10000.0) * index * (2.0 / HD)).astype(np.float32)[None, :]
    any_space = pl.BlockSpec(memory_space=pl.ANY)
    vmem = pl.BlockSpec(memory_space=pltpu.VMEM)
    dma = pltpu.SemaphoreType.DMA
    return pl.pallas_call(
        kernel,
        out_shape=jax.ShapeDtypeStruct((MINE, ROWS), BF),
        in_specs=[any_space, vmem, any_space, any_space, any_space, vmem],
        out_specs=vmem,
        scratch_shapes=[
            pltpu.VMEM((NK, ROWS, KC), BF),
            pltpu.VMEM((NK, ROWS, KC), BF),
            pltpu.VMEM((D, HD), BF),
            pltpu.VMEM((NK, KC, 2 * HD), BF),
            pltpu.VMEM((HD, D), BF),
            pltpu.VMEM((D, HD), BF),
            pltpu.VMEM((NZ + 1, FEATS, HD), BF),
            pltpu.VMEM((2, 3 * ROWS, HD), BF),
            pltpu.VMEM((ROWS, HD), BF),
            pltpu.VMEM((NB, NZ, BLK, HD), BF),
            pltpu.VMEM((ROWS, 2 * HD), F32),
            pltpu.VMEM((ROWS, HD), F32),
            pltpu.VMEM((ROWS, HD), F32),
            pltpu.VMEM((ROWS, HD), F32),
            pltpu.VMEM((NB, MINE, BLK), BF),
            pltpu.VMEM((NB, MINE, BLK), BF),
            pltpu.VMEM((NB, MINE, BLK), F32),
            pltpu.VMEM((NB, BLK, HD), BF),
            dma((NK,)), dma((NK,)), dma, dma,
            dma((NB,)), dma((NB,)), dma((NB,)), dma((NB,)),
            dma((1,)), dma((1,)), dma((2, NB)), dma((2, NB)),
            dma((HALF,)), dma((HALF,)), dma((NX,)), dma((NX,)), dma((NX,)), dma((NX,)),
            dma((NB, HALF)), dma((NB, HALF)), dma((NB, NZ)), dma((NB,)), dma((NB,)),
            dma((2, NB)), dma((NB,)),
        ],
        compiler_params=pltpu.CompilerParams(
            collective_id=0, has_side_effects=True, vmem_limit_bytes=60 * 1024 * 1024
        ),
    )(
        hidden_in, norm_gain, query_weight, kv_weight, out_weight, jnp.asarray(freq),
    )


def solution(mesh):
    in_specs = (P("seq", None), P(), P(None, "mp"), P(None, "mp"), P("mp", None))
    out_specs = P("mp", "seq")
    return jax.shard_map(
        per_device, mesh=mesh, in_specs=in_specs, out_specs=out_specs, check_vma=False
    )
```
